256 devices in a mesh: seq: 32 (over z, y), head: 8 (over x, core).
Axes of the slice: x: 4, y: 4, z: 8, core: 2. Of those that a mesh axis runs over, the one named last changes fastest.
Arguments:
- inputs: bfloat16 [32768, 5120], P('seq', 'head'), may hold values from -0.59765625 to 0.59765625
- gates: bfloat16 [32768, 5120], P('seq', 'head'), may hold values from -6 to 6
- write_keys: bfloat16 [32768, 128], P('seq'), may hold values from -6 to 6
- read_keys: bfloat16 [32768, 128], P('seq'), may hold values from -0.125 to 0.125
- log_decay: float32 [80, 32768], P('head', 'seq'), may hold values from -3 to 0
- skip_gain: float32 [80], P('head'), may hold values from 0.5 to 4
- doc_ids: int32 [32768], P('seq'), may hold values from 0 to 3, never falling along the last dimension, each value on 1 to 16384 neighbouring positions
- out_weight: bfloat16 [5120, 2560], P('head'), may hold values from -0.078125 to 0.078125
- grad_out: bfloat16 [32768, 2560], P(('seq', 'head')), may hold values from -6 to 6
Outputs:
- mixed_out: bfloat16 [32768, 2560], P(('seq', 'head'))
- grad_inputs: bfloat16 [32768, 5120], P('seq', 'head')
The draws below stay inside these ranges and needn't reach their ends.
Inputs may be any that keep to these rules, and one draw needn't show every extreme that they name: `doc_ids`: document ids never fall along the sequence; every document has 1 to 16384 tokens and one has exactly 16384.
All inputs are finite; a program needn't handle non-finite values.
Results may differ from the reference program's by a relative error of at most 0.02.
Values may be sent and summed in bfloat16 or wider, within the bound.
A program may use at most 128 MiB of HBM per device.

```python
import math
import jax
import jax.numpy as jnp
import numpy as np
from jax import lax

D = 2560
H = 80
P_SIZE = 64
N = 128
GROUP = 256
TOK_DEV = 1024
DOCS = 4
PACKED_TOKENS = 32768


def draw_log_decay(key, part):
    key_rows = jax.random.split(key, 7)
    slow_share = 0.5
    slow_heads = jax.random.uniform(key_rows[0], (H,)) < slow_share
    fast_rate = jnp.exp(jax.random.uniform(key_rows[1], (H,), minval=math.log(1.0 / 50.0), maxval=math.log(1.0 / 30.0)))
    slow_rate = jnp.exp(jax.random.uniform(key_rows[2], (H,), minval=math.log(0.2), maxval=math.log(0.8))) / PACKED_TOKENS
    head_decay_rate = jnp.where(slow_heads, slow_rate, fast_rate)
    shard_factor = jax.random.uniform(key_rows[3], (H, PACKED_TOKENS // TOK_DEV), minval=0.6, maxval=1.4)
    shard_complete = jnp.repeat(shard_factor, TOK_DEV, axis=1)
    token_multiplier = jax.random.uniform(key_rows[4], (H, PACKED_TOKENS), minval=0.5, maxval=1.5)
    segment_location = jax.random.randint(key_rows[5], (4,), 0, PACKED_TOKENS)
    segment_depth = jax.random.uniform(key_rows[6], (4,), minval=math.log(0.5), maxval=math.log(0.8))
    segment_runs = jnp.zeros((PACKED_TOKENS,), jnp.float32).at[segment_location].add(segment_depth)
    value_rows = -head_decay_rate[:, None] * shard_complete * token_multiplier + segment_runs[None, :]
    return value_rows.astype(jnp.float32)


def block_levels(own_key, extent, cuts, low, largest):
    gain = 1.0
    for position, blocks in cuts:
        steps = jax.random.uniform(jax.random.fold_in(jax.random.fold_in(own_key, 6), position), (blocks,), jnp.float32, low / len(cuts), largest / len(cuts))
        gain = gain * jnp.repeat(jnp.exp(steps), extent[position] // blocks).reshape((-1,) + (1,) * (len(extent) - 1 - position))
    return gain


def profile(count, total, bound, lean):
    weights = [(1 << 20) // math.isqrt(standing ** lean) + 1 for standing in range(2, count + 1)]
    surplus, holding = total - bound - (count - 1), [1] * (count - 1)
    while surplus > 0:
        free = [i for i in range(count - 1) if holding[i] < bound]
        mass, remaining = sum([weights[i] for i in free]), surplus
        for i in free:
            extra = min(bound - holding[i], max(1, remaining * weights[i] // mass), surplus)
            holding[i] = holding[i] + extra
            surplus = surplus - extra
    return np.array([bound] + holding)


def ragged_sizes(stream_key, number_of, total, most, slope):
    if number_of == 2:
        one = jax.random.randint(stream_key, (), max(1, total - most), min(most, total - 1) + 1)
        return jnp.stack([one, total - one])
    tallies = jnp.asarray(profile(number_of, total, most, slope), jnp.int32)
    twos = (number_of - 1) // 2
    donor, receiver = tallies[1:1 + 2 * twos:2], tallies[2:2 + 2 * twos:2]
    margin = jnp.minimum(donor - 1, most - receiver)
    passed = jax.random.randint(jax.random.fold_in(stream_key, 1), (twos,), 0, 1 << 20) % (margin + 1)
    tallies = tallies.at[1:1 + 2 * twos:2].set(donor - passed).at[2:2 + 2 * twos:2].set(receiver + passed)
    return tallies[jax.random.permutation(jax.random.fold_in(stream_key, 2), number_of)]


def normal_values(stream_key, extent, width, most, cuts=(), held_as=jnp.bfloat16):
    result = width * jax.random.normal(stream_key, extent, jnp.float32)
    if cuts:
        result = result * block_levels(stream_key, extent, cuts, -0.22, 0.18)
    return jnp.clip(result, -most, most).astype(held_as)


def setup_inputs(seed: int = 0) -> dict:
    key_of = jax.random.split(jax.random.key(seed), 10)
    return {
        "inputs": normal_values(key_of[0], (PACKED_TOKENS, H * P_SIZE), 0.1, 0.59765625, ((0, 32), (1, 8))),
        "gates": normal_values(key_of[1], (PACKED_TOKENS, H * P_SIZE), 1.0, 6.0, ((0, 32), (1, 8))),
        "write_keys": normal_values(key_of[2], (PACKED_TOKENS, N), 1.0, 6.0, ((0, 32),)),
        "read_keys": normal_values(key_of[3], (PACKED_TOKENS, N), (16 * N) ** -0.5, 0.125, ((0, 32),)),
        "log_decay": draw_log_decay(jax.random.fold_in(key_of[9], 71), 0),
        "skip_gain": jnp.clip(jnp.exp(math.log(4.0) - 2.0794415 * jax.random.uniform(key_of[5], (H,), jnp.float32) ** block_levels(key_of[5], (H,), ((0, 8),), -0.2, 0.2)), 0.5, 4.0),
        "doc_ids": jnp.searchsorted(jnp.cumsum(ragged_sizes(key_of[6], DOCS, PACKED_TOKENS, PACKED_TOKENS // 2, 0)), jnp.arange(PACKED_TOKENS), side="right").astype(jnp.int32),
        "out_weight": normal_values(key_of[7], (H * P_SIZE, D), (H * P_SIZE) ** -0.5, 0.078125, ((0, 8),)),
        "grad_out": normal_values(key_of[8], (PACKED_TOKENS, D), 1.0, 6.0, ((0, 256),)),
    }


def group_terms(write_blk, read_blk, decay_blk, doc_blk, before):
    block_len = doc_blk.shape[0]
    cumul = jnp.cumsum(decay_blk, axis=1)
    positions = jnp.arange(block_len)
    causal_same = (doc_blk[:, None] == doc_blk[None, :]) & (positions[:, None] >= positions[None, :])
    spread = jnp.where(causal_same[None], cumul[:, :, None] - cumul[:, None, :], 0.0)
    decay_matrix = jnp.where(causal_same[None], jnp.exp(spread), 0.0)
    scores = jnp.dot(read_blk, write_blk.T, preferred_element_type=jnp.float32)
    weights = (decay_matrix * scores[None]).astype(jnp.bfloat16)
    entry_w = jnp.where((doc_blk == before)[None], jnp.exp(cumul), 0.0)
    exit_w = jnp.where((doc_blk == doc_blk[block_len - 1])[None], jnp.exp(cumul[:, block_len - 1:] - cumul), 0.0)
    return weights, entry_w, exit_w, entry_w[:, block_len - 1]


def reference(inputs, gates, write_keys, read_keys, log_decay, skip_gain, doc_ids, out_weight, grad_out):
    tok_total, inner = inputs.shape
    head_count = log_decay.shape[0]
    head_width = inner // head_count
    state_width = write_keys.shape[1]
    group_count = tok_total // GROUP
    blocks_x = inputs.reshape(group_count, GROUP, head_count, head_width)
    blocks_b = write_keys.reshape(group_count, GROUP, state_width)
    blocks_c = read_keys.reshape(group_count, GROUP, state_width)
    blocks_d = log_decay.reshape(head_count, group_count, GROUP).transpose(1, 0, 2)
    doc_blocks = doc_ids.reshape(group_count, GROUP)
    befores = jnp.concatenate([jnp.full((1,), -1, jnp.int32), doc_blocks[:-1, GROUP - 1]])
    silu_gate = jax.nn.silu(gates.astype(jnp.float32))
    gate_blocks = silu_gate.reshape(group_count, GROUP, head_count, head_width)
    skip_full = skip_gain[None, :, None]
    empty_state = jnp.zeros((head_count, head_width, state_width), jnp.float32)

    def forward(entering, blk):
        x_blk, write_blk, read_blk, decay_blk, doc_blk, before, gate_blk = blk
        weights, entry_w, exit_w, block_decay = group_terms(write_blk, read_blk, decay_blk, doc_blk, before)
        inner_part = jnp.einsum('hts,shp->thp', weights.astype(jnp.float32), x_blk.astype(jnp.float32))
        rounded = lax.optimization_barrier(entering.astype(jnp.bfloat16)).astype(jnp.float32)
        carried = jnp.einsum('tn,hpn->thp', read_blk.astype(jnp.float32), rounded) * entry_w.T[:, :, None]
        mixed = inner_part + carried + skip_full * x_blk.astype(jnp.float32)
        gated = (mixed * gate_blk).astype(jnp.bfloat16)
        write_scaled = (exit_w.T[:, :, None] * x_blk.astype(jnp.float32)).astype(jnp.bfloat16)
        own_state = jnp.einsum('shp,sn->hpn', write_scaled.astype(jnp.float32), write_blk.astype(jnp.float32))
        return block_decay[:, None, None] * entering + own_state, gated

    _, gated_blocks = lax.scan(forward, empty_state, (blocks_x, blocks_b, blocks_c, blocks_d, doc_blocks, befores, gate_blocks))
    gated_all = gated_blocks.reshape(tok_total, inner)
    mixed_out = jnp.dot(gated_all, out_weight, preferred_element_type=jnp.float32).astype(jnp.bfloat16)

    grad_gated = jnp.dot(grad_out, out_weight.T, preferred_element_type=jnp.float32)
    grad_mix = (grad_gated * silu_gate).astype(jnp.bfloat16)
    blocks_dy = grad_mix.reshape(group_count, GROUP, head_count, head_width)

    def backward(arriving, blk):
        dy_blk, write_blk, read_blk, decay_blk, doc_blk, before = blk
        weights, entry_w, exit_w, block_decay = group_terms(write_blk, read_blk, decay_blk, doc_blk, before)
        inner_part = jnp.einsum('hts,thp->shp', weights.astype(jnp.float32), dy_blk.astype(jnp.float32))
        rounded = lax.optimization_barrier(arriving.astype(jnp.bfloat16)).astype(jnp.float32)
        carried = jnp.einsum('sn,hpn->shp', write_blk.astype(jnp.float32), rounded) * exit_w.T[:, :, None]
        grad_blk = (inner_part + carried + skip_full * dy_blk.astype(jnp.float32)).astype(jnp.bfloat16)
        grad_scaled = (entry_w.T[:, :, None] * dy_blk.astype(jnp.float32)).astype(jnp.bfloat16)
        own_state = jnp.einsum('thp,tn->hpn', grad_scaled.astype(jnp.float32), read_blk.astype(jnp.float32))
        return own_state + block_decay[:, None, None] * arriving, grad_blk

    _, grad_blocks = lax.scan(backward, empty_state, (blocks_dy, blocks_b, blocks_c, blocks_d, doc_blocks, befores), reverse=True)
    return mixed_out, grad_blocks.reshape(tok_total, inner)
```

```python
import math

import jax
import jax.numpy as jnp
from jax import lax
from jax.experimental import pallas as pl
from jax.experimental.pallas import tpu as pltpu
from jax.sharding import PartitionSpec as P

NX, NY, NZ = 4, 4, 8
Q = 128
CHUNKS = 8
TOK = Q * CHUNKS
HEADS = 10
PAIRS = 5
HP = 64
WIDTH = HEADS * HP
N = 128
D = 2560
QR = N // NY
HALF = 64
LOG2E = 1.0 / math.log(2.0)
MESH = pl.DeviceIdType.MESH
BF = jnp.bfloat16
F32 = jnp.float32


def dot(a, b):
    return jnp.dot(a, b, preferred_element_type=F32)


def dot_nt(a, b):
    return lax.dot_general(a, b, (((1,), (1,)), ((), ())), preferred_element_type=F32)


def dot_tn(a, b):
    return lax.dot_general(a, b, (((0,), (0,)), ((), ())), preferred_element_type=F32)


def split3(v):
    a = v.astype(BF)
    rest = v - a.astype(F32)
    b = rest.astype(BF)
    return a, b, (rest - b.astype(F32)).astype(BF)


def stacked(rows, count):
    place = lax.broadcasted_iota(jnp.int32, (count, 128), 0)
    out = jnp.zeros((count, 128), F32)
    for k, row in enumerate(rows):
        out = jnp.where(place == k, row, out)
    return out


def kernel(
    x_hbm, g_hbm, wk, rk, ld, skip, docs, wo_hbm, go_hbm,
    mo, gi,
    x_v, g_v, wo_v, go_v, silu_v, mix_v, gl_v, exc_v, enc_v, exs_v, ens_v, wt_v, dy_v,
    enter_v, arr_v, own_v, run_v, ldp_v, ccol_v, crow_v, dt_v, bd_v, off_v, prev_v, spread_v,
    y1s, y1r, m1s, m1r, zs, zr, mzs, mzr, y2s, y2r, wrow_v, brow_v, zrow_v,
    b1s, b1r, bzs, bzr, b2s, b2r,
    pall, pr, qs, rla, rlb, fl, fr,
    lsem, agx_s, agx_r, agd_s, agd_r,
    y1_ss, y1_rs, m1_ss, m1_rs, z_ss, z_rs, mz_ss, mz_rs, y2_ss, y2_rs,
    b1_ss, b1_rs, bz_ss, bz_rs, b2_ss, b2_rs,
    d_ss, d_rs, rx_ss, rx_rs,
):
    seq = lax.axis_index("seq")
    head = lax.axis_index("head")
    z, y = seq // NY, seq % NY
    xx, core = head // 2, head % 2
    x_at = lambda k: (xx + k) % NX

    def dev(seq_id, head_id):
        return {"seq": seq_id, "head": head_id}

    right = dev(seq, x_at(1) * 2 + core)
    left = dev(seq, x_at(3) * 2 + core)
    partner = dev(seq, xx * 2 + 1 - core)
    y_peer = lambda r: dev(z * NY + (y + r) % NY, head)
    z_peer = lambda r: dev(((z + r) % NZ) * NY + y, head)

    def remote(src, dst, ss, rs, to):
        return pltpu.make_async_remote_copy(
            src_ref=src, dst_ref=dst, send_sem=ss, recv_sem=rs, device_id=to, device_id_type=MESH
        )

    started = []

    def send(*args):
        copy = remote(*args)
        copy.start()
        started.append(copy)

    own_rows = pl.ds(pl.multiple_of(head * Q, Q), Q)
    loads = [
        pltpu.make_async_copy(go_hbm, go_v.at[own_rows, :], lsem.at[0]),
        pltpu.make_async_copy(x_hbm, x_v, lsem.at[1]),
        pltpu.make_async_copy(g_hbm, g_v, lsem.at[2]),
        pltpu.make_async_copy(wo_hbm, wo_v, lsem.at[3]),
    ]
    for copy in loads:
        copy.start()

    barrier = pltpu.get_barrier_semaphore()
    peers = [right, left, partner]
    peers += [y_peer(r) for r in range(1, NY)] + [z_peer(r) for r in range(1, NZ)]
    for peer in peers:
        pl.semaphore_signal(barrier, inc=1, device_id=peer, device_id_type=MESH)
    pl.semaphore_wait(barrier, len(peers))

    def go_rows(place, of_core, half):
        start = pl.multiple_of((place * 2 + of_core) * Q + half * HALF, HALF)
        return go_v.at[pl.ds(start, HALF), :]

    loads[0].wait()
    for half in (0, 1):
        ref = go_rows(xx, core, half)
        send(ref, ref, agx_s.at[half], agx_r.at[half], right)
    for half in (1, 0):
        ref = go_rows(xx, core, half)
        send(ref, ref, agx_s.at[2 + half], agx_r.at[2 + half], left)
    own_ref = go_v.at[own_rows, :]
    send(own_ref, own_ref, agd_s.at[6], agd_r.at[6], partner)

    def ag_got(unit):
        place = x_at((3, 3, 1, 1, 2, 2)[unit])
        ref = go_rows(place, core, unit % 2)
        remote(ref, ref, agx_s.at[unit], agx_r.at[unit], left).wait_recv()
        if unit == 0:
            send(ref, ref, agx_s.at[4], agx_r.at[4], right)
        if unit == 3:
            send(ref, ref, agx_s.at[5], agx_r.at[5], left)
        send(ref, ref, agd_s.at[unit], agd_r.at[unit], partner)

    def ag_pair_got(unit):
        place = x_at((3, 3, 1, 1, 2, 2)[unit])
        ref = go_rows(place, 1 - core, unit % 2)
        remote(ref, ref, agd_s.at[unit], agd_r.at[unit], partner).wait_recv()

    sub = lax.broadcasted_iota(jnp.int32, (Q, Q), 0)
    lane = lax.broadcasted_iota(jnp.int32, (Q, Q), 1)
    tri = (lane <= sub).astype(F32).astype(BF)
    eye = (lane == sub).astype(F32).astype(BF)
    head_lane = lax.broadcasted_iota(jnp.int32, (1, 128), 1)
    lane_row = (lax.broadcasted_iota(jnp.int32, (128, WIDTH), 1) // HP)
    head_row = lax.broadcasted_iota(jnp.int32, (128, WIDTH), 0)
    spread_v[...] = (lane_row == head_row).astype(F32).astype(BF)
    m_lo = (head_lane < HP).astype(F32).astype(BF)
    m_hi = (head_lane >= HP).astype(F32).astype(BF)

    def expand(w):
        return dot(w.astype(BF), spread_v[...])

    def expand_fine(w):
        a = w.astype(BF)
        return dot(a, spread_v[...]) + dot((w - a.astype(F32)).astype(BF), spread_v[...])

    def rows_of(c):
        return pl.ds(pl.multiple_of(c * Q, Q), Q)

    ldp_v[...] = jnp.zeros_like(ldp_v)
    ldp_v[0:HEADS, :] = ld[...] * LOG2E
    doc_f = docs[...].astype(F32)
    df = jnp.broadcast_to(doc_f[0:1, 0:1], (1, 128))
    off_v[...] = jnp.zeros_like(off_v)
    prev_v[...] = jnp.broadcast_to(df, prev_v.shape)
    run_v[...] = jnp.zeros_like(run_v)
    loads[1].wait()

    @pl.loop(0, CHUNKS)
    def _(c):
        rows = rows_of(c)
        cols = rows_of(c)
        parts = split3(ldp_v[:, cols])
        ccol = sum(dot_nt(tri, part) for part in parts)
        ccol_v[rows, :] = ccol
        crow_v[c] = sum(dot_nt(part[0:16], tri) for part in parts)
        doc_row = docs[pl.ds(c, 1), :].astype(F32)
        dt = dot_nt(eye, jnp.broadcast_to(doc_row, (Q, Q)).astype(BF))
        dt_v[rows, :] = dt
        c_end, d_end = ccol[Q - 1 : Q, :], dt[Q - 1 : Q, :]
        exc = expand(jnp.where(dt == d_end, jnp.exp2(c_end - ccol), 0.0)).astype(BF)
        exc_v[rows, :] = exc
        prev = prev_v[0:1, :]
        bd = jnp.where(d_end == prev, jnp.exp2(c_end), 0.0)
        bdx = expand_fine(jnp.broadcast_to(bd, (8, 128)))
        bd_v[c] = bdx
        own = dot_tn(wk[rows, :], x_v[rows, :] * exc)
        run = run_v[...]
        enter_v[c] = run.astype(BF)
        run_v[...] = run * bdx[0:1, :] + own
        entw = jnp.where(dt == prev, jnp.exp2(ccol), 0.0)
        enc_v[rows, :] = expand(entw).astype(BF)
        off = off_v[0:1, :]
        ens_v[rows, :] = expand(jnp.where(dt == df, jnp.exp2(ccol + off), 0.0)).astype(BF)
        prev_v[...] = jnp.broadcast_to(d_end, prev_v.shape)
        off_v[...] = jnp.broadcast_to(off + c_end, off_v.shape)

    total = off_v[0:1, :]
    dl = prev_v[0:1, :]
    y1s[...] = run_v[...].astype(BF)
    m1s[...] = stacked([total, df, dl], 8)
    own_q = pl.ds(pl.multiple_of(y * QR, QR), QR)
    m1r[y] = m1s[...]
    y1r[y] = y1s[own_q, :]
    for r in range(1, NY):
        q_rows = pl.ds(pl.multiple_of(((y + r) % NY) * QR, QR), QR)
        send(m1s, m1r.at[y], m1_ss.at[r], m1_rs.at[r], y_peer(r))
        send(y1s.at[q_rows, :], y1r.at[y], y1_ss.at[r], y1_rs.at[r], y_peer(r))

    skip_rows = [
        jnp.where(head_lane < HP, skip[2 * p], skip[2 * p + 1]) for p in range(PAIRS)
    ]

    def pair(p):
        return slice(p * 128, (p + 1) * 128)

    def doubled(v):
        return jnp.concatenate([v * m_lo, v * m_hi], axis=0)

    def inner_chunk(c):
        rows = rows_of(c)
        ccol, dt = ccol_v[rows, :], dt_v[rows, :]
        crow = crow_v[c]
        same = dt == docs[pl.ds(c, 1), :].astype(F32)
        b, k = wk[rows, :], rk[rows, :]
        sm = jnp.where(same & (sub >= lane), dot_nt(k, b), 0.0)
        stm = jnp.where(same & (lane >= sub), dot_nt(b, k), 0.0)
        off_c = off_v[0:1, :]
        shard_c = ccol + off_c
        exs = jnp.where(dt == dl, jnp.exp2(total - shard_c), 0.0)
        exs_v[rows, :] = expand(exs).astype(BF)
        for p in range(PAIRS):
            ws, wts = [], []
            for h in (2 * p, 2 * p + 1):
                gap = ccol[:, h : h + 1] - crow[h : h + 1, :]
                ws.append((jnp.exp2(jnp.minimum(gap, 0.0)) * sm).astype(BF))
                wts.append((jnp.exp2(jnp.minimum(-gap, 0.0)) * stm).astype(BF))
            wt_v[c, p] = jnp.concatenate(wts, axis=1)
            xp = x_v[rows, pair(p)]
            mixed = dot(jnp.concatenate(ws, axis=1), doubled(xp))
            mixed += enc_v[rows, pair(p)].astype(F32) * dot(k, enter_v[c, :, pair(p)])
            mix_v[rows, pair(p)] = mixed + skip_rows[p] * xp.astype(F32)
            gate = g_v[rows, pair(p)].astype(F32)
            silu_v[rows, pair(p)] = gate / (1.0 + jnp.exp(-gate))
        off_v[...] = jnp.broadcast_to(off_c + ccol[Q - 1 : Q, :], off_v.shape)

    off_v[...] = jnp.zeros_like(off_v)
    loads[2].wait()
    pl.loop(0, 4)(inner_chunk)

    for r in range(1, NY):
        source = (y + NY - r) % NY
        remote(m1s, m1r.at[source], m1_ss.at[r], m1_rs.at[r], y_peer(r)).wait_recv()
        remote(y1s.at[own_q, :], y1r.at[source], y1_ss.at[r], y1_rs.at[r], y_peer(r)).wait_recv()
    meta = [m1r[j] for j in range(NY)]
    ls = [m[0:1, :] for m in meta]
    dfs = [m[1:2, :] for m in meta]
    dls = [m[2:3, :] for m in meta]

    def span(values):
        out = jnp.zeros((1, 128), F32)
        for v in values:
            out = out + v
        return out

    def gated_decay(a, b, values):
        return jnp.where(a == b, jnp.exp2(span(values)), 0.0)

    t_rows = [gated_decay(dls[j], dls[NY - 1], ls[j + 1 :]) for j in range(NY)]
    t_rows += [gated_decay(dfs[j], dfs[0], ls[:j]) for j in range(NY)]
    zrow_v[...] = expand_fine(stacked(t_rows, 8))
    zs[...] = sum(zrow_v[j : j + 1, :] * y1r[j].astype(F32) for j in range(NY)).astype(BF)
    mzs[...] = stacked([span(ls), dfs[0], dls[NY - 1]], 8)
    zr[z] = zs[...]
    mzr[z] = mzs[...]
    for r in range(1, NZ):
        send(mzs, mzr.at[z], mz_ss.at[r], mz_rs.at[r], z_peer(r))
        send(zs, zr.at[z], z_ss.at[r], z_rs.at[r], z_peer(r))

    in_row = [(j, k) for k in range(NY) for j in range(k)]
    f_rows = [gated_decay(dls[j], dfs[k], ls[j + 1 : k]) for j, k in in_row]
    f_rows += [gated_decay(dfs[0], dfs[k], ls[:k]) for k in range(NY)]
    wrow_v[...] = expand_fine(stacked(f_rows, 16))
    b_rows = [gated_decay(dfs[k], dls[j], ls[j + 1 : k]) for j, k in in_row]
    b_rows += [gated_decay(dls[NY - 1], dls[k], ls[k + 1 :]) for k in range(NY)]
    brow_v[...] = expand_fine(stacked(b_rows, 16))

    ag_got(0)
    ag_got(3)

    pl.loop(4, CHUNKS)(inner_chunk)

    loads[3].wait()

    def grad_mix_of(place):
        rows = pl.ds(pl.multiple_of(place * 2 * Q, 2 * Q), 2 * Q)
        grad = dot_nt(go_v[rows, :], wo_v[...])
        dy_v[rows, :] = (grad * silu_v[rows, :]).astype(BF)
        for k in (0, 1):
            c = place * 2 + k
            one = rows_of(c)
            own_v[c] = dot_tn(rk[one, :], dy_v[one, :] * enc_v[one, :])

    pair_own = go_v.at[pl.ds(pl.multiple_of((xx * 2 + 1 - core) * Q, Q), Q), :]
    remote(pair_own, pair_own, agd_s.at[6], agd_r.at[6], partner).wait_recv()
    grad_mix_of(xx)

    ag_got(1)
    ag_got(2)

    for r in range(1, NZ):
        source = (z + NZ - r) % NZ
        remote(mzs, mzr.at[source], mz_ss.at[r], mz_rs.at[r], z_peer(r)).wait_recv()
        remote(zs, zr.at[source], z_ss.at[r], z_rs.at[r], z_peer(r)).wait_recv()
    zmeta = [mzr[i] for i in range(NZ)]
    rls = [m[0:1, :] for m in zmeta]
    rdfs = [m[1:2, :] for m in zmeta]
    rdls = [m[2:3, :] for m in zmeta]

    def flag(condition):
        return jnp.where(condition, 1.0, 0.0).astype(F32)

    zf_rows, zb_rows = [], []
    for i in range(NZ):
        gap = span([rls[m] * flag(m < z) for m in range(i + 1, NZ)])
        zf_rows.append(flag(i < z) * jnp.where(rdls[i] == dfs[0], jnp.exp2(gap), 0.0))
        gap = span([rls[m] * flag(m > z) for m in range(i)])
        zb_rows.append(flag(i > z) * jnp.where(rdfs[i] == dls[NY - 1], jnp.exp2(gap), 0.0))
    zf = expand_fine(stacked(zf_rows, 8))
    row_state = sum(zf[i : i + 1, :] * zr[i].astype(F32) for i in range(NZ))
    for k in range(NY):
        out = wrow_v[6 + k : 7 + k, :] * row_state
        for place, (j, kk) in enumerate(in_row):
            if kk == k:
                out += wrow_v[place : place + 1, :] * y1r[j].astype(F32)
        y2s[k * QR : (k + 1) * QR, :] = out.astype(BF)
    y2r[own_q, :] = y2s[own_q, :]
    for r in range(1, NY):
        q_rows = pl.ds(pl.multiple_of(((y + r) % NY) * QR, QR), QR)
        send(y2s.at[q_rows, :], y2r.at[own_q, :], y2_ss.at[r], y2_rs.at[r], y_peer(r))
    zrow_b = expand_fine(stacked(zb_rows, 8))

    ag_pair_got(0)
    ag_pair_got(1)
    grad_mix_of(x_at(3))
    ag_pair_got(2)
    ag_pair_got(3)
    grad_mix_of(x_at(1))

    for r in range(1, NY):
        source = pl.ds(pl.multiple_of(((y + NY - r) % NY) * QR, QR), QR)
        remote(y2s.at[own_q, :], y2r.at[source, :], y2_ss.at[r], y2_rs.at[r], y_peer(r)).wait_recv()

    order = [x_at(2), x_at(1), x_at(3), xx]
    mine = pl.ds(pl.multiple_of(core * Q, Q), Q)
    theirs = pl.ds(pl.multiple_of((1 - core) * Q, Q), Q)

    def project(k):
        rows = pl.ds(pl.multiple_of(order[k] * 2 * Q, 2 * Q), 2 * Q)
        carried = ens_v[rows, :].astype(F32) * dot(rk[rows, :], y2r[...])
        gated = ((mix_v[rows, :] + carried) * silu_v[rows, :]).astype(BF)
        for n in range(5):
            cols = slice(n * 512, (n + 1) * 512)
            pall[k, :, cols] = dot(gated, wo_v[:, cols]).astype(BF)
        send(pall.at[k, theirs, :], pr.at[k], d_ss.at[k], d_rs.at[k], partner)

    def pair_sum(k, start, count):
        rows = pl.ds(pl.multiple_of(core * Q + start, HALF), count)
        return pall[k, rows, :].astype(F32) + pr[k, start : start + count, :].astype(F32)

    def pair_got(k):
        remote(pall.at[k, mine, :], pr.at[k], d_ss.at[k], d_rs.at[k], partner).wait_recv()

    def half(ref, which):
        return ref.at[pl.ds(which * HALF, HALF), :]

    project(0)
    project(1)
    pair_got(0)
    qs[0] = pair_sum(0, 0, Q).astype(BF)
    send(half(qs.at[0], 0), rla, rx_ss.at[0], rx_rs.at[0], right)
    send(half(qs.at[0], 1), rlb, rx_ss.at[1], rx_rs.at[1], left)
    project(2)
    pair_got(1)
    qs[1, HALF:Q, :] = pair_sum(1, HALF, HALF).astype(BF)
    send(half(qs.at[1], 1), half(fl, 1), rx_ss.at[2], rx_rs.at[2], right)
    pair_got(2)
    qs[2, 0:HALF, :] = pair_sum(2, 0, HALF).astype(BF)
    send(half(qs.at[2], 0), half(fr, 0), rx_ss.at[3], rx_rs.at[3], left)

    ag_got(4)
    ag_got(5)
    ag_pair_got(4)
    ag_pair_got(5)
    grad_mix_of(x_at(2))
    run_v[...] = jnp.zeros_like(run_v)

    @pl.loop(0, CHUNKS)
    def _(back):
        c = CHUNKS - 1 - back
        run = run_v[...]
        arr_v[c] = run.astype(BF)
        run_v[...] = own_v[c] + bd_v[c, 0:1, :] * run

    b1s[...] = run_v[...].astype(BF)
    b1r[y] = b1s[own_q, :]
    for r in range(1, NY):
        q_rows = pl.ds(pl.multiple_of(((y + r) % NY) * QR, QR), QR)
        send(b1s.at[q_rows, :], b1r.at[y], b1_ss.at[r], b1_rs.at[r], y_peer(r))

    project(3)

    def relay():
        remote(half(qs.at[0], 0), rla, rx_ss.at[0], rx_rs.at[0], right).wait_recv()
        qs[1, 0:HALF, :] = (pair_sum(1, 0, HALF) + rla[...].astype(F32)).astype(BF)
        send(half(qs.at[1], 0), half(fl, 0), rx_ss.at[4], rx_rs.at[4], right)
        remote(half(qs.at[0], 1), rlb, rx_ss.at[1], rx_rs.at[1], left).wait_recv()
        qs[2, HALF:Q, :] = (pair_sum(2, HALF, HALF) + rlb[...].astype(F32)).astype(BF)
        send(half(qs.at[2], 1), half(fr, 1), rx_ss.at[5], rx_rs.at[5], left)

    def grad_chunk(c):
        rows = rows_of(c)
        b = wk[rows, :]
        for p in range(PAIRS):
            dyp = dy_v[rows, pair(p)]
            grad = dot(wt_v[c, p], doubled(dyp))
            grad += exc_v[rows, pair(p)].astype(F32) * dot(b, arr_v[c, :, pair(p)])
            gl_v[rows, pair(p)] = grad + skip_rows[p] * dyp.astype(F32)

    pl.loop(0, 4)(grad_chunk)

    for r in range(1, NY):
        source = (y + NY - r) % NY
        remote(b1s.at[own_q, :], b1r.at[source], b1_ss.at[r], b1_rs.at[r], y_peer(r)).wait_recv()
    bzs[...] = sum(
        zrow_v[NY + j : NY + j + 1, :] * b1r[j].astype(F32) for j in range(NY)
    ).astype(BF)
    bzr[z] = bzs[...]
    for r in range(1, NZ):
        send(bzs, bzr.at[z], bz_ss.at[r], bz_rs.at[r], z_peer(r))

    relay()
    pl.loop(4, CHUNKS)(grad_chunk)

    for r in range(1, NZ):
        source = (z + NZ - r) % NZ
        remote(bzs, bzr.at[source], bz_ss.at[r], bz_rs.at[r], z_peer(r)).wait_recv()
    row_state = sum(zrow_b[i : i + 1, :] * bzr[i].astype(F32) for i in range(NZ))
    for k in range(NY):
        out = brow_v[6 + k : 7 + k, :] * row_state
        for place, (kk, j) in enumerate(in_row):
            if kk == k:
                out += brow_v[place : place + 1, :] * b1r[j].astype(F32)
        b2s[k * QR : (k + 1) * QR, :] = out.astype(BF)
    b2r[own_q, :] = b2s[own_q, :]
    for r in range(1, NY):
        q_rows = pl.ds(pl.multiple_of(((y + r) % NY) * QR, QR), QR)
        send(b2s.at[q_rows, :], b2r.at[own_q, :], b2_ss.at[r], b2_rs.at[r], y_peer(r))

    pair_got(3)
    qs[3] = pair_sum(3, 0, Q).astype(BF)

    for r in range(1, NY):
        source = pl.ds(pl.multiple_of(((y + NY - r) % NY) * QR, QR), QR)
        remote(b2s.at[own_q, :], b2r.at[source, :], b2_ss.at[r], b2_rs.at[r], y_peer(r)).wait_recv()

    @pl.loop(0, CHUNKS)
    def _(c):
        rows = rows_of(c)
        carried = exs_v[rows, :].astype(F32) * dot(wk[rows, :], b2r[...])
        gi[rows, :] = (gl_v[rows, :] + carried).astype(BF)

    remote(half(qs.at[1], 1), half(fl, 1), rx_ss.at[2], rx_rs.at[2], right).wait_recv()
    remote(half(qs.at[2], 0), half(fr, 0), rx_ss.at[3], rx_rs.at[3], left).wait_recv()
    remote(half(qs.at[1], 0), half(fl, 0), rx_ss.at[4], rx_rs.at[4], right).wait_recv()
    remote(half(qs.at[2], 1), half(fr, 1), rx_ss.at[5], rx_rs.at[5], left).wait_recv()
    mo[...] = (qs[3].astype(F32) + fl[...].astype(F32) + fr[...].astype(F32)).astype(BF)

    for copy in started:
        copy.wait_send()


def shards(
    inputs, gates, write_keys, read_keys, log_decay, skip_gain, doc_ids, out_weight, grad_out
):
    vmem = pl.BlockSpec(memory_space=pltpu.VMEM)
    smem = pl.BlockSpec(memory_space=pltpu.SMEM)
    hbm = pl.BlockSpec(memory_space=pl.ANY)
    v = lambda shape, kind=BF: pltpu.VMEM(shape, kind)
    dma = lambda *shape: pltpu.SemaphoreType.DMA(shape)
    full = (TOK, WIDTH)
    scratch = [
        v(full), v(full), v((WIDTH, D)), v((TOK, D)), v(full, F32), v(full, F32), v(full, F32),
        v(full), v(full), v(full), v(full), v((CHUNKS, PAIRS, Q, 2 * Q)), v(full),
        v((CHUNKS, N, WIDTH)), v((CHUNKS, N, WIDTH)), v((CHUNKS, N, WIDTH), F32),
        v((N, WIDTH), F32), v((128, TOK), F32), v((TOK, 128), F32), v((CHUNKS, 16, Q), F32),
        v((TOK, 128), F32), v((CHUNKS, 8, WIDTH), F32), v((8, 128), F32), v((8, 128), F32),
        v((128, WIDTH)),
        v((N, WIDTH)), v((NY, QR, WIDTH)), v((8, 128), F32), v((NY, 8, 128), F32),
        v((QR, WIDTH)), v((NZ, QR, WIDTH)), v((8, 128), F32), v((NZ, 8, 128), F32),
        v((N, WIDTH)), v((N, WIDTH)), v((16, WIDTH), F32), v((16, WIDTH), F32),
        v((8, WIDTH), F32),
        v((N, WIDTH)), v((NY, QR, WIDTH)), v((QR, WIDTH)), v((NZ, QR, WIDTH)),
        v((N, WIDTH)), v((N, WIDTH)),
        v((NX, 2 * Q, D)), v((NX, Q, D)), v((NX, Q, D)), v((HALF, D)), v((HALF, D)),
        v((Q, D)), v((Q, D)),
        dma(4), dma(6), dma(6), dma(7), dma(7),
        dma(NY), dma(NY), dma(NY), dma(NY), dma(NZ), dma(NZ), dma(NZ), dma(NZ), dma(NY), dma(NY),
        dma(NY), dma(NY), dma(NZ), dma(NZ), dma(NY), dma(NY),
        dma(4), dma(4), dma(6), dma(6),
    ]
    return pl.pallas_call(
        kernel,
        out_shape=(
            jax.ShapeDtypeStruct((Q, D), BF),
            jax.ShapeDtypeStruct((TOK, WIDTH), BF),
        ),
        in_specs=[hbm, hbm, vmem, vmem, vmem, smem, vmem, hbm, hbm],
        out_specs=(vmem, vmem),
        scratch_shapes=scratch,
        compiler_params=pltpu.CompilerParams(
            collective_id=0, has_side_effects=True, vmem_limit_bytes=60 * 1024 * 1024
        ),
    )(
        inputs, gates, write_keys, read_keys, log_decay, skip_gain,
        doc_ids.reshape(CHUNKS, Q), out_weight, grad_out,
    )


def solution(mesh):
    return jax.shard_map(
        shards,
        mesh=mesh,
        in_specs=(
            P("seq", "head"),
            P("seq", "head"),
            P("seq", None),
            P("seq", None),
            P("head", "seq"),
            P("head"),
            P("seq"),
            P("head", None),
            P(("seq", "head"), None),
        ),
        out_specs=(P(("seq", "head"), None), P("seq", "head")),
        check_vma=False,
    )
```

```python
import math

import jax
import jax.numpy as jnp
from jax import lax
from jax.experimental import pallas as pl
from jax.experimental.pallas import tpu as pltpu
from jax.sharding import PartitionSpec as P

NX, NY, NZ = 4, 4, 8
Q = 128
CHUNKS = 8
TOK = Q * CHUNKS
HEADS = 10
PAIRS = 5
HP = 64
WIDTH = HEADS * HP
N = 128
D = 2560
QR = N // NY
HALF = 64
LOG2E = 1.0 / math.log(2.0)
MESH = pl.DeviceIdType.MESH
BF = jnp.bfloat16
F32 = jnp.float32


def dot(a, b):
    return jnp.dot(a, b, preferred_element_type=F32)


def dot_nt(a, b):
    return lax.dot_general(a, b, (((1,), (1,)), ((), ())), preferred_element_type=F32)


def dot_tn(a, b):
    return lax.dot_general(a, b, (((0,), (0,)), ((), ())), preferred_element_type=F32)


def split3(v):
    a = v.astype(BF)
    rest = v - a.astype(F32)
    b = rest.astype(BF)
    return a, b, (rest - b.astype(F32)).astype(BF)


def stacked(rows, count):
    place = lax.broadcasted_iota(jnp.int32, (count, 128), 0)
    out = jnp.zeros((count, 128), F32)
    for k, row in enumerate(rows):
        out = jnp.where(place == k, row, out)
    return out


def kernel(
    x_hbm, g_hbm, wk_hbm, rk_hbm, ld, skip, docs, wo_hbm, go_hbm,
    mo, gi,
    x_v, g_v, wk, rk, wo_v, go_v, silu_v, mix_v, gl_v, exc_v, enc_v, exs_v, ens_v, wt_v, dy_v,
    enter_v, arr_v, own_v, run_v, ldp_v, docm_v, ccol_v, crow_v, wexc_v, wenc_v, wens_v, bd_v,
    spread_v,
    y1s, y1r, m1s, m1r, zs, zr, mzs, mzr, y2s, y2r, wrow_v, brow_v, zrow_v,
    b1s, b1r, bzs, bzr, b2s, b2r,
    pall, pr, qs, rla, rlb, fl, fr,
    lsem, agx_s, agx_r, agd_s, agd_r,
    y1_ss, y1_rs, m1_ss, m1_rs, z_ss, z_rs, mz_ss, mz_rs, y2_ss, y2_rs,
    b1_ss, b1_rs, bz_ss, bz_rs, b2_ss, b2_rs,
    d_ss, d_rs, rx_ss, rx_rs,
):
    seq = lax.axis_index("seq")
    head = lax.axis_index("head")
    z, y = seq // NY, seq % NY
    xx, core = head // 2, head % 2
    x_at = lambda k: (xx + k) % NX

    def dev(seq_id, head_id):
        return {"seq": seq_id, "head": head_id}

    right = dev(seq, x_at(1) * 2 + core)
    left = dev(seq, x_at(3) * 2 + core)
    partner = dev(seq, xx * 2 + 1 - core)
    y_peer = lambda r: dev(z * NY + (y + r) % NY, head)
    z_peer = lambda r: dev(((z + r) % NZ) * NY + y, head)

    def remote(src, dst, ss, rs, to):
        return pltpu.make_async_remote_copy(
            src_ref=src, dst_ref=dst, send_sem=ss, recv_sem=rs, device_id=to, device_id_type=MESH
        )

    started = []

    def send(*args):
        copy = remote(*args)
        copy.start()
        started.append(copy)

    own_rows = pl.ds(pl.multiple_of(head * Q, Q), Q)
    loads = [
        pltpu.make_async_copy(x_hbm, x_v, lsem.at[0]),
        pltpu.make_async_copy(wk_hbm, wk, lsem.at[1]),
        pltpu.make_async_copy(rk_hbm, rk, lsem.at[2]),
        pltpu.make_async_copy(g_hbm, g_v, lsem.at[3]),
        pltpu.make_async_copy(go_hbm, go_v.at[own_rows, :], lsem.at[4]),
        pltpu.make_async_copy(wo_hbm, wo_v, lsem.at[5]),
    ]

    barrier = pltpu.get_barrier_semaphore()
    peers = [right, left, partner]
    peers += [y_peer(r) for r in range(1, NY)] + [z_peer(r) for r in range(1, NZ)]
    for peer in peers:
        pl.semaphore_signal(barrier, inc=1, device_id=peer, device_id_type=MESH)
    for copy in loads:
        copy.start()

    sub = lax.broadcasted_iota(jnp.int32, (Q, Q), 0)
    lane = lax.broadcasted_iota(jnp.int32, (Q, Q), 1)
    ones = lambda condition: condition.astype(F32).astype(BF)
    tri = ones(lane <= sub)
    eye = ones(lane == sub)
    head_lane = lax.broadcasted_iota(jnp.int32, (1, 128), 1)
    same_head = (sub % 16) == (lane % 16)
    head_of = lax.broadcasted_iota(jnp.int32, (128, WIDTH), 1) // HP
    spread_v[...] = ones(head_of == lax.broadcasted_iota(jnp.int32, (128, WIDTH), 0) % 16)
    m_lo = ones(head_lane < HP)
    m_hi = ones(head_lane >= HP)

    def in_block(c):
        return ones(head_lane // 16 == c)

    def expand_row(w):
        w = jnp.where(head_lane < 16, w, 0.0)
        a = w.astype(BF)
        return dot(a, spread_v[...]) + dot((w - a.astype(F32)).astype(BF), spread_v[...])

    def rows_of(c):
        return pl.ds(pl.multiple_of(c * Q, Q), Q)

    ldp_v[...] = jnp.zeros_like(ldp_v)
    for c in range(CHUNKS):
        ldp_v[16 * c : 16 * c + HEADS, :] = ld[:, c * Q : (c + 1) * Q] * LOG2E
        docm_v[16 * c : 16 * c + 16, :] = jnp.broadcast_to(docs[c : c + 1, :].astype(F32), (16, Q))
    parts = split3(ldp_v[...])
    ccol_all = sum(dot_nt(tri, part) for part in parts)
    ccol_v[...] = ccol_all
    dt_all = dot_nt(eye, docm_v[...].astype(BF))
    c_end, d_end = ccol_all[Q - 1 : Q, :], dt_all[Q - 1 : Q, :]
    df = jnp.broadcast_to(docm_v[0:1, 0:1], (1, 128))
    dl = jnp.broadcast_to(docm_v[127:128, 127:128], (1, 128))
    end_parts = split3(jnp.broadcast_to(c_end, (8, 128)))
    before = ones(same_head & (sub // 16 < lane // 16))
    off = sum(dot(part, before) for part in end_parts)[0:1, :]
    total = sum(dot(part, ones(same_head)) for part in end_parts)[0:1, :]
    prev = jnp.where(head_lane < 16, df, pltpu.roll(d_end, 16, 1))
    w_exs = jnp.where(dt_all == dl, jnp.exp2(total - off - ccol_all), 0.0).astype(BF)

    pl.semaphore_wait(barrier, len(peers))

    def go_rows(place, of_core, half):
        start = pl.multiple_of((place * 2 + of_core) * Q + half * HALF, HALF)
        return go_v.at[pl.ds(start, HALF), :]

    for half in (0, 1):
        part = go_hbm.at[pl.ds(half * HALF, HALF), :]
        send(part, go_rows(xx, core, half), agx_s.at[half], agx_r.at[half], right)
        part = go_hbm.at[pl.ds((1 - half) * HALF, HALF), :]
        send(part, go_rows(xx, core, 1 - half), agx_s.at[3 - half], agx_r.at[3 - half], left)
    send(go_hbm, go_v.at[own_rows, :], agd_s.at[6], agd_r.at[6], partner)

    def ag_got(unit):
        place = x_at((3, 3, 1, 1, 2, 2)[unit])
        ref = go_rows(place, core, unit % 2)
        remote(ref, ref, agx_s.at[unit], agx_r.at[unit], left).wait_recv()
        if unit == 0:
            send(ref, ref, agx_s.at[4], agx_r.at[4], right)
        if unit == 3:
            send(ref, ref, agx_s.at[5], agx_r.at[5], left)
        send(ref, ref, agd_s.at[unit], agd_r.at[unit], partner)

    def ag_pair_got(unit):
        place = x_at((3, 3, 1, 1, 2, 2)[unit])
        ref = go_rows(place, 1 - core, unit % 2)
        remote(ref, ref, agd_s.at[unit], agd_r.at[unit], partner).wait_recv()

    loads[0].wait()
    for c in range(CHUNKS):
        rows = slice(c * Q, (c + 1) * Q)
        exs = dot(w_exs * in_block(c), spread_v[...]).astype(BF)
        exs_v[rows, :] = exs
        dy_v[rows, :] = x_v[rows, :] * exs
    loads[1].wait()
    y1s[...] = dot_tn(wk[...], dy_v[...]).astype(BF)
    m1s[...] = stacked([total, df, dl], 8)
    own_q = pl.ds(pl.multiple_of(y * QR, QR), QR)
    m1r[y] = m1s[...]
    y1r[y] = y1s[own_q, :]
    for r in range(1, NY):
        q_rows = pl.ds(pl.multiple_of(((y + r) % NY) * QR, QR), QR)
        send(m1s, m1r.at[y], m1_ss.at[r], m1_rs.at[r], y_peer(r))
        send(y1s.at[q_rows, :], y1r.at[y], y1_ss.at[r], y1_rs.at[r], y_peer(r))

    skip_rows = [
        jnp.where(head_lane < HP, skip[2 * p], skip[2 * p + 1]) for p in range(PAIRS)
    ]

    def pair(p):
        return slice(p * 128, (p + 1) * 128)

    def doubled(v):
        return jnp.concatenate([v * m_lo, v * m_hi], axis=0)

    crow_v[...] = sum(dot_nt(part, tri) for part in parts)
    wexc_v[...] = jnp.where(dt_all == d_end, jnp.exp2(c_end - ccol_all), 0.0).astype(BF)
    wenc_v[...] = jnp.where(dt_all == prev, jnp.exp2(ccol_all), 0.0).astype(BF)
    wens_v[...] = jnp.where(dt_all == df, jnp.exp2(ccol_all + off), 0.0).astype(BF)
    block_decay = jnp.where(d_end == prev, jnp.exp2(c_end), 0.0)
    of_block = lax.broadcasted_iota(jnp.int32, (CHUNKS, 128), 0) == (
        lax.broadcasted_iota(jnp.int32, (CHUNKS, 128), 1) // 16
    )
    block_decay = jnp.where(of_block, block_decay, 0.0)
    coarse = block_decay.astype(BF)
    fine = (block_decay - coarse.astype(F32)).astype(BF)
    bd_v[...] = dot(coarse, spread_v[...]) + dot(fine, spread_v[...])
    run_v[...] = jnp.zeros_like(run_v)

    def inner_chunk(c):
        rows = rows_of(c)
        mine_only = in_block(c)
        exc = dot(wexc_v[...] * mine_only, spread_v[...]).astype(BF)
        exc_v[rows, :] = exc
        enc = dot(wenc_v[...] * mine_only, spread_v[...])
        enc_v[rows, :] = enc.astype(BF)
        ens_v[rows, :] = dot(wens_v[...] * mine_only, spread_v[...]).astype(BF)
        run = run_v[...]
        enter_v[c] = run.astype(BF)
        b, k = wk[rows, :], rk[rows, :]
        run_v[...] = run * bd_v[pl.ds(c, 1), :] + dot_tn(b, x_v[rows, :] * exc)
        ccol = pltpu.roll(ccol_v[...], (128 - 16 * c) % 128, 1)
        crow = crow_v[pl.ds(pl.multiple_of(c * 16, 16), 16), :]
        doc_row = docs[pl.ds(c, 1), :].astype(F32)
        dt = dot_nt(eye, jnp.broadcast_to(doc_row, (Q, Q)).astype(BF))
        same = dt == doc_row
        sm = jnp.where(same & (sub >= lane), dot_nt(k, b), 0.0)
        stm = jnp.where(same & (lane >= sub), dot_nt(b, k), 0.0)
        for p in range(PAIRS):
            ws, wts = [], []
            for h in (2 * p, 2 * p + 1):
                gap = ccol[:, h : h + 1] - crow[h : h + 1, :]
                ws.append((jnp.exp2(jnp.minimum(gap, 0.0)) * sm).astype(BF))
                wts.append((jnp.exp2(jnp.minimum(-gap, 0.0)) * stm).astype(BF))
            wt_v[c, p] = jnp.concatenate(wts, axis=1)
            xp = x_v[rows, pair(p)]
            mixed = dot(jnp.concatenate(ws, axis=1), doubled(xp))
            mixed += enc_v[rows, pair(p)].astype(F32) * dot(k, enter_v[c, :, pair(p)])
            mix_v[rows, pair(p)] = mixed + skip_rows[p] * xp.astype(F32)
            gate = g_v[rows, pair(p)].astype(F32)
            silu_v[rows, pair(p)] = gate / (1.0 + jnp.exp(-gate))

    loads[2].wait()
    loads[3].wait()
    pl.loop(0, 4)(inner_chunk)

    for r in range(1, NY):
        source = (y + NY - r) % NY
        remote(m1s, m1r.at[source], m1_ss.at[r], m1_rs.at[r], y_peer(r)).wait_recv()
        remote(y1s.at[own_q, :], y1r.at[source], y1_ss.at[r], y1_rs.at[r], y_peer(r)).wait_recv()
    meta = [m1r[j] for j in range(NY)]
    ls = [m[0:1, :] for m in meta]
    dfs = [m[1:2, :] for m in meta]
    dls = [m[2:3, :] for m in meta]

    def span(values):
        out = jnp.zeros((1, 128), F32)
        for v in values:
            out = out + v
        return out

    def gated_decay(a, b, values):
        return jnp.where(a == b, jnp.exp2(span(values)), 0.0)

    t_rows = [gated_decay(dls[j], dls[NY - 1], ls[j + 1 :]) for j in range(NY)]
    t_rows += [gated_decay(dfs[j], dfs[0], ls[:j]) for j in range(NY)]
    zrow_v[...] = expand_row(stacked(t_rows, 8))
    zs[...] = sum(zrow_v[j : j + 1, :] * y1r[j].astype(F32) for j in range(NY)).astype(BF)
    mzs[...] = stacked([span(ls), dfs[0], dls[NY - 1]], 8)
    zr[z] = zs[...]
    mzr[z] = mzs[...]
    for r in range(1, NZ):
        send(mzs, mzr.at[z], mz_ss.at[r], mz_rs.at[r], z_peer(r))
        send(zs, zr.at[z], z_ss.at[r], z_rs.at[r], z_peer(r))

    in_row = [(j, k) for k in range(NY) for j in range(k)]
    f_rows = [gated_decay(dls[j], dfs[k], ls[j + 1 : k]) for j, k in in_row]
    f_rows += [gated_decay(dfs[0], dfs[k], ls[:k]) for k in range(NY)]
    wrow_v[...] = expand_row(stacked(f_rows, 16))
    b_rows = [gated_decay(dfs[k], dls[j], ls[j + 1 : k]) for j, k in in_row]
    b_rows += [gated_decay(dls[NY - 1], dls[k], ls[k + 1 :]) for k in range(NY)]
    brow_v[...] = expand_row(stacked(b_rows, 16))

    ag_got(0)
    ag_got(3)

    pl.loop(4, CHUNKS)(inner_chunk)

    loads[4].wait()
    loads[5].wait()

    def grad_mix_of(place):
        rows = pl.ds(pl.multiple_of(place * 2 * Q, 2 * Q), 2 * Q)
        grad = dot_nt(go_v[rows, :], wo_v[...])
        dy_v[rows, :] = (grad * silu_v[rows, :]).astype(BF)
        for k in (0, 1):
            c = place * 2 + k
            one = rows_of(c)
            own_v[c] = dot_tn(rk[one, :], dy_v[one, :] * enc_v[one, :])

    pair_own = go_v.at[pl.ds(pl.multiple_of((xx * 2 + 1 - core) * Q, Q), Q), :]
    remote(pair_own, pair_own, agd_s.at[6], agd_r.at[6], partner).wait_recv()
    grad_mix_of(xx)

    ag_got(1)
    ag_got(2)
    ag_pair_got(0)
    ag_pair_got(1)
    grad_mix_of(x_at(3))

    for r in range(1, NZ):
        source = (z + NZ - r) % NZ
        remote(mzs, mzr.at[source], mz_ss.at[r], mz_rs.at[r], z_peer(r)).wait_recv()
        remote(zs, zr.at[source], z_ss.at[r], z_rs.at[r], z_peer(r)).wait_recv()
    zmeta = [mzr[i] for i in range(NZ)]
    rls = [m[0:1, :] for m in zmeta]
    rdfs = [m[1:2, :] for m in zmeta]
    rdls = [m[2:3, :] for m in zmeta]

    def flag(condition):
        return jnp.where(condition, 1.0, 0.0).astype(F32)

    zf_rows, zb_rows = [], []
    for i in range(NZ):
        gap = span([rls[m] * flag(m < z) for m in range(i + 1, NZ)])
        zf_rows.append(flag(i < z) * jnp.where(rdls[i] == dfs[0], jnp.exp2(gap), 0.0))
        gap = span([rls[m] * flag(m > z) for m in range(i)])
        zb_rows.append(flag(i > z) * jnp.where(rdfs[i] == dls[NY - 1], jnp.exp2(gap), 0.0))
    zf = expand_row(stacked(zf_rows, 8))
    row_state = sum(zf[i : i + 1, :] * zr[i].astype(F32) for i in range(NZ))
    for k in range(NY):
        out = wrow_v[6 + k : 7 + k, :] * row_state
        for place, (j, kk) in enumerate(in_row):
            if kk == k:
                out += wrow_v[place : place + 1, :] * y1r[j].astype(F32)
        y2s[k * QR : (k + 1) * QR, :] = out.astype(BF)
    y2r[own_q, :] = y2s[own_q, :]
    for r in range(1, NY):
        q_rows = pl.ds(pl.multiple_of(((y + r) % NY) * QR, QR), QR)
        send(y2s.at[q_rows, :], y2r.at[own_q, :], y2_ss.at[r], y2_rs.at[r], y_peer(r))
    zrow_b = expand_row(stacked(zb_rows, 8))

    ag_pair_got(2)
    ag_pair_got(3)
    grad_mix_of(x_at(1))
    ag_got(4)
    ag_got(5)

    for r in range(1, NY):
        source = pl.ds(pl.multiple_of(((y + NY - r) % NY) * QR, QR), QR)
        remote(y2s.at[own_q, :], y2r.at[source, :], y2_ss.at[r], y2_rs.at[r], y_peer(r)).wait_recv()

    order = [x_at(2), x_at(1), x_at(3), xx]
    mine = pl.ds(pl.multiple_of(core * Q, Q), Q)
    theirs = pl.ds(pl.multiple_of((1 - core) * Q, Q), Q)

    def project(k):
        rows = pl.ds(pl.multiple_of(order[k] * 2 * Q, 2 * Q), 2 * Q)
        carried = ens_v[rows, :].astype(F32) * dot(rk[rows, :], y2r[...])
        gated = ((mix_v[rows, :] + carried) * silu_v[rows, :]).astype(BF)
        for n in range(5):
            cols = slice(n * 512, (n + 1) * 512)
            pall[k, :, cols] = dot(gated, wo_v[:, cols]).astype(BF)
        send(pall.at[k, theirs, :], pr.at[k], d_ss.at[k], d_rs.at[k], partner)

    def pair_sum(k, start, count):
        rows = pl.ds(pl.multiple_of(core * Q + start, HALF), count)
        return pall[k, rows, :].astype(F32) + pr[k, start : start + count, :].astype(F32)

    def pair_got(k):
        remote(pall.at[k, mine, :], pr.at[k], d_ss.at[k], d_rs.at[k], partner).wait_recv()

    def half(ref, which):
        return ref.at[pl.ds(which * HALF, HALF), :]

    project(0)
    project(1)
    pair_got(0)
    qs[0] = pair_sum(0, 0, Q).astype(BF)
    send(half(qs.at[0], 0), rla, rx_ss.at[0], rx_rs.at[0], right)
    send(half(qs.at[0], 1), rlb, rx_ss.at[1], rx_rs.at[1], left)

    ag_pair_got(4)
    ag_pair_got(5)
    grad_mix_of(x_at(2))
    run_v[...] = jnp.zeros_like(run_v)

    @pl.loop(0, CHUNKS)
    def _(back):
        c = CHUNKS - 1 - back
        run = run_v[...]
        arr_v[c] = run.astype(BF)
        run_v[...] = own_v[c] + bd_v[pl.ds(c, 1), :] * run

    b1s[...] = run_v[...].astype(BF)
    b1r[y] = b1s[own_q, :]
    for r in range(1, NY):
        q_rows = pl.ds(pl.multiple_of(((y + r) % NY) * QR, QR), QR)
        send(b1s.at[q_rows, :], b1r.at[y], b1_ss.at[r], b1_rs.at[r], y_peer(r))

    pair_got(1)
    qs[1, HALF:Q, :] = pair_sum(1, HALF, HALF).astype(BF)
    send(half(qs.at[1], 1), half(fl, 1), rx_ss.at[2], rx_rs.at[2], right)
    project(2)
    project(3)
    pair_got(2)
    qs[2, 0:HALF, :] = pair_sum(2, 0, HALF).astype(BF)
    send(half(qs.at[2], 0), half(fr, 0), rx_ss.at[3], rx_rs.at[3], left)

    def relay():
        remote(half(qs.at[0], 0), rla, rx_ss.at[0], rx_rs.at[0], right).wait_recv()
        qs[1, 0:HALF, :] = (pair_sum(1, 0, HALF) + rla[...].astype(F32)).astype(BF)
        send(half(qs.at[1], 0), half(fl, 0), rx_ss.at[4], rx_rs.at[4], right)
        remote(half(qs.at[0], 1), rlb, rx_ss.at[1], rx_rs.at[1], left).wait_recv()
        qs[2, HALF:Q, :] = (pair_sum(2, HALF, HALF) + rlb[...].astype(F32)).astype(BF)
        send(half(qs.at[2], 1), half(fr, 1), rx_ss.at[5], rx_rs.at[5], left)

    def grad_chunk(c):
        rows = rows_of(c)
        b = wk[rows, :]
        for p in range(PAIRS):
            dyp = dy_v[rows, pair(p)]
            grad = dot(wt_v[c, p], doubled(dyp))
            grad += exc_v[rows, pair(p)].astype(F32) * dot(b, arr_v[c, :, pair(p)])
            gl_v[rows, pair(p)] = grad + skip_rows[p] * dyp.astype(F32)

    pl.loop(0, 4)(grad_chunk)

    for r in range(1, NY):
        source = (y + NY - r) % NY
        remote(b1s.at[own_q, :], b1r.at[source], b1_ss.at[r], b1_rs.at[r], y_peer(r)).wait_recv()
    bzs[...] = sum(
        zrow_v[NY + j : NY + j + 1, :] * b1r[j].astype(F32) for j in range(NY)
    ).astype(BF)
    bzr[z] = bzs[...]
    for r in range(1, NZ):
        send(bzs, bzr.at[z], bz_ss.at[r], bz_rs.at[r], z_peer(r))

    relay()
    pl.loop(4, CHUNKS)(grad_chunk)

    for r in range(1, NZ):
        source = (z + NZ - r) % NZ
        remote(bzs, bzr.at[source], bz_ss.at[r], bz_rs.at[r], z_peer(r)).wait_recv()
    row_state = sum(zrow_b[i : i + 1, :] * bzr[i].astype(F32) for i in range(NZ))
    for k in range(NY):
        out = brow_v[6 + k : 7 + k, :] * row_state
        for place, (kk, j) in enumerate(in_row):
            if kk == k:
                out += brow_v[place : place + 1, :] * b1r[j].astype(F32)
        b2s[k * QR : (k + 1) * QR, :] = out.astype(BF)
    b2r[own_q, :] = b2s[own_q, :]
    for r in range(1, NY):
        q_rows = pl.ds(pl.multiple_of(((y + r) % NY) * QR, QR), QR)
        send(b2s.at[q_rows, :], b2r.at[own_q, :], b2_ss.at[r], b2_rs.at[r], y_peer(r))

    pair_got(3)
    qs[3] = pair_sum(3, 0, Q).astype(BF)

    for r in range(1, NY):
        source = pl.ds(pl.multiple_of(((y + NY - r) % NY) * QR, QR), QR)
        remote(b2s.at[own_q, :], b2r.at[source, :], b2_ss.at[r], b2_rs.at[r], y_peer(r)).wait_recv()

    @pl.loop(0, CHUNKS)
    def _(c):
        rows = rows_of(c)
        carried = exs_v[rows, :].astype(F32) * dot(wk[rows, :], b2r[...])
        gi[rows, :] = (gl_v[rows, :] + carried).astype(BF)

    remote(half(qs.at[1], 1), half(fl, 1), rx_ss.at[2], rx_rs.at[2], right).wait_recv()
    remote(half(qs.at[2], 0), half(fr, 0), rx_ss.at[3], rx_rs.at[3], left).wait_recv()
    remote(half(qs.at[1], 0), half(fl, 0), rx_ss.at[4], rx_rs.at[4], right).wait_recv()
    remote(half(qs.at[2], 1), half(fr, 1), rx_ss.at[5], rx_rs.at[5], left).wait_recv()
    mo[...] = (qs[3].astype(F32) + fl[...].astype(F32) + fr[...].astype(F32)).astype(BF)

    for copy in started:
        copy.wait_send()


def write_out(mo, gi, mo_out, gi_out, sem):
    copies = [
        pltpu.make_async_copy(mo, mo_out, sem.at[0]),
        pltpu.make_async_copy(gi, gi_out, sem.at[1]),
    ]
    for copy in copies:
        copy.start()
    for copy in copies:
        copy.wait()


def shards(
    inputs, gates, write_keys, read_keys, log_decay, skip_gain, doc_ids, out_weight, grad_out
):
    vmem = pl.BlockSpec(memory_space=pltpu.VMEM)
    smem = pl.BlockSpec(memory_space=pltpu.SMEM)
    hbm = pl.BlockSpec(memory_space=pl.ANY)
    v = lambda shape, kind=BF: pltpu.VMEM(shape, kind)
    dma = lambda *shape: pltpu.SemaphoreType.DMA(shape)
    full, square = (TOK, WIDTH), (128, 128)
    scratch = [
        v(full), v(full), v((TOK, N)), v((TOK, N)), v((WIDTH, D)), v((TOK, D)),
        v(full, F32), v(full, F32), v(full, F32),
        v(full), v(full), v(full), v(full), v((CHUNKS, PAIRS, Q, 2 * Q)), v(full),
        v((CHUNKS, N, WIDTH)), v((CHUNKS, N, WIDTH)), v((CHUNKS, N, WIDTH), F32),
        v((N, WIDTH), F32), v(square, F32), v(square, F32), v(square, F32), v(square, F32),
        v(square), v(square), v(square), v((CHUNKS, WIDTH), F32),
        v((128, WIDTH)),
        v((N, WIDTH)), v((NY, QR, WIDTH)), v((8, 128), F32), v((NY, 8, 128), F32),
        v((QR, WIDTH)), v((NZ, QR, WIDTH)), v((8, 128), F32), v((NZ, 8, 128), F32),
        v((N, WIDTH)), v((N, WIDTH)), v((16, WIDTH), F32), v((16, WIDTH), F32),
        v((8, WIDTH), F32),
        v((N, WIDTH)), v((NY, QR, WIDTH)), v((QR, WIDTH)), v((NZ, QR, WIDTH)),
        v((N, WIDTH)), v((N, WIDTH)),
        v((NX, 2 * Q, D)), v((NX, Q, D)), v((NX, Q, D)), v((HALF, D)), v((HALF, D)),
        v((Q, D)), v((Q, D)),
        dma(6), dma(6), dma(6), dma(7), dma(7),
        dma(NY), dma(NY), dma(NY), dma(NY), dma(NZ), dma(NZ), dma(NZ), dma(NZ), dma(NY), dma(NY),
        dma(NY), dma(NY), dma(NZ), dma(NZ), dma(NY), dma(NY),
        dma(4), dma(4), dma(6), dma(6),
    ]
    results = pl.pallas_call(
        kernel,
        out_shape=(pltpu.VMEM((Q, D), BF), pltpu.VMEM((TOK, WIDTH), BF)),
        in_specs=[hbm, hbm, hbm, hbm, vmem, smem, vmem, hbm, hbm],
        out_specs=(vmem, vmem),
        scratch_shapes=scratch,
        compiler_params=pltpu.CompilerParams(
            collective_id=0, has_side_effects=True, vmem_limit_bytes=54 * 1024 * 1024
        ),
    )(
        inputs, gates, write_keys, read_keys, log_decay, skip_gain,
        doc_ids.reshape(CHUNKS, Q), out_weight, grad_out,
    )
    return pl.pallas_call(
        write_out,
        out_shape=(
            jax.ShapeDtypeStruct((Q, D), BF),
            jax.ShapeDtypeStruct((TOK, WIDTH), BF),
        ),
        in_specs=[vmem, vmem],
        out_specs=(hbm, hbm),
        scratch_shapes=[dma(2)],
        compiler_params=pltpu.CompilerParams(vmem_limit_bytes=1024 * 1024),
    )(*results)


def solution(mesh):
    return jax.shard_map(
        shards,
        mesh=mesh,
        in_specs=(
            P("seq", "head"),
            P("seq", "head"),
            P("seq", None),
            P("seq", None),
            P("head", "seq"),
            P("head"),
            P("seq"),
            P("head", None),
            P(("seq", "head"), None),
        ),
        out_specs=(P(("seq", "head"), None), P("seq", "head")),
        check_vma=False,
    )
```

```python
import math

import jax
import jax.numpy as jnp
from jax import lax
from jax.experimental import pallas as pl
from jax.experimental.pallas import tpu as pltpu
from jax.sharding import PartitionSpec as P

NX, NY, NZ = 4, 4, 8
Q = 128
CHUNKS = 8
TOK = Q * CHUNKS
HEADS = 10
PAIRS = 5
HP = 64
WIDTH = HEADS * HP
N = 128
D = 2560
QR = N // NY
HALF = 64
LOG2E = 1.0 / math.log(2.0)
MESH = pl.DeviceIdType.MESH
BF = jnp.bfloat16
F32 = jnp.float32


def dot(a, b):
    return jnp.dot(a, b, preferred_element_type=F32)


def dot_nt(a, b):
    return lax.dot_general(a, b, (((1,), (1,)), ((), ())), preferred_element_type=F32)


def dot_tn(a, b):
    return lax.dot_general(a, b, (((0,), (0,)), ((), ())), preferred_element_type=F32)


def split3(v):
    a = v.astype(BF)
    rest = v - a.astype(F32)
    b = rest.astype(BF)
    return a, b, (rest - b.astype(F32)).astype(BF)


def stacked(rows, count):
    place = lax.broadcasted_iota(jnp.int32, (count, 128), 0)
    out = jnp.zeros((count, 128), F32)
    for k, row in enumerate(rows):
        out = jnp.where(place == k, row, out)
    return out


def kernel(
    x_hbm, g_hbm, wk_hbm, rk_hbm, ld, skip, docs, wo_hbm, go_hbm,
    mo, gi,
    x_v, g_v, wk, rk, wo_v, go_v, silu_v, mix_v, gl_v, exc_v, enc_v, exs_v, ens_v, wt_v, dy_v,
    enter_v, arr_v, gsum_v, run_v, ldp_v, docm_v, ccol_v, crow_v, wexc_v, wenc_v, wens_v, bd_v,
    spread_v,
    y1s, y1r, m1s, m1r, zs, zr, mzs, mzr, y2s, y2r, wrow_v, brow_v, zrow_v,
    b1s, b1r, bzs, bzr, b2s, b2r,
    pall, pr, qs, rla, rlb, fl, fr,
    lsem, agx_s, agx_r, agd_s, agd_r,
    y1_ss, y1_rs, m1_ss, m1_rs, z_ss, z_rs, mz_ss, mz_rs, y2_ss, y2_rs,
    b1_ss, b1_rs, bz_ss, bz_rs, b2_ss, b2_rs,
    d_ss, d_rs, rx_ss, rx_rs,
):
    seq = lax.axis_index("seq")
    head = lax.axis_index("head")
    z, y = seq // NY, seq % NY
    xx, core = head // 2, head % 2
    x_at = lambda k: (xx + k) % NX

    def dev(seq_id, head_id):
        return {"seq": seq_id, "head": head_id}

    right = dev(seq, x_at(1) * 2 + core)
    left = dev(seq, x_at(3) * 2 + core)
    partner = dev(seq, xx * 2 + 1 - core)
    y_peer = lambda r: dev(z * NY + (y + r) % NY, head)
    z_peer = lambda r: dev(((z + r) % NZ) * NY + y, head)

    def remote(src, dst, ss, rs, to):
        return pltpu.make_async_remote_copy(
            src_ref=src, dst_ref=dst, send_sem=ss, recv_sem=rs, device_id=to, device_id_type=MESH
        )

    started = []

    def send(*args):
        copy = remote(*args)
        copy.start()
        started.append(copy)

    own_rows = pl.ds(pl.multiple_of(head * Q, Q), Q)
    loads = [
        pltpu.make_async_copy(x_hbm, x_v, lsem.at[0]),
        pltpu.make_async_copy(wk_hbm, wk, lsem.at[1]),
        pltpu.make_async_copy(rk_hbm, rk, lsem.at[2]),
        pltpu.make_async_copy(g_hbm, g_v, lsem.at[3]),
        pltpu.make_async_copy(go_hbm, go_v.at[own_rows, :], lsem.at[4]),
        pltpu.make_async_copy(wo_hbm, wo_v, lsem.at[5]),
    ]

    barrier = pltpu.get_barrier_semaphore()
    peers = [right, left, partner]
    peers += [y_peer(r) for r in range(1, NY)] + [z_peer(r) for r in range(1, NZ)]
    for peer in peers:
        pl.semaphore_signal(barrier, inc=1, device_id=peer, device_id_type=MESH)
    for copy in loads:
        copy.start()
    pl.semaphore_wait(barrier, len(peers))

    def go_rows(place, of_core, half):
        start = pl.multiple_of((place * 2 + of_core) * Q + half * HALF, HALF)
        return go_v.at[pl.ds(start, HALF), :]

    for half in (0, 1):
        part = go_hbm.at[pl.ds(half * HALF, HALF), :]
        send(part, go_rows(xx, core, half), agx_s.at[half], agx_r.at[half], right)
        part = go_hbm.at[pl.ds((1 - half) * HALF, HALF), :]
        send(part, go_rows(xx, core, 1 - half), agx_s.at[3 - half], agx_r.at[3 - half], left)
    send(go_hbm, go_v.at[own_rows, :], agd_s.at[6], agd_r.at[6], partner)

    sub = lax.broadcasted_iota(jnp.int32, (Q, Q), 0)
    lane = lax.broadcasted_iota(jnp.int32, (Q, Q), 1)
    ones = lambda condition: condition.astype(F32).astype(BF)
    tri = ones(lane <= sub)
    eye = ones(lane == sub)
    head_lane = lax.broadcasted_iota(jnp.int32, (1, 128), 1)
    same_head = (sub % 16) == (lane % 16)
    head_of = lax.broadcasted_iota(jnp.int32, (128, WIDTH), 1) // HP
    spread_v[...] = ones(head_of == lax.broadcasted_iota(jnp.int32, (128, WIDTH), 0) % 16)
    m_lo = ones(head_lane < HP)
    m_hi = ones(head_lane >= HP)

    def in_block(c):
        return ones(head_lane // 16 == c)

    def expand_row(w):
        w = jnp.where(head_lane < 16, w, 0.0)
        a = w.astype(BF)
        return dot(a, spread_v[...]) + dot((w - a.astype(F32)).astype(BF), spread_v[...])

    def rows_of(c):
        return pl.ds(pl.multiple_of(c * Q, Q), Q)

    ldp_v[...] = jnp.zeros_like(ldp_v)
    for c in range(CHUNKS):
        ldp_v[16 * c : 16 * c + HEADS, :] = ld[:, c * Q : (c + 1) * Q] * LOG2E
        docm_v[16 * c : 16 * c + 16, :] = jnp.broadcast_to(docs[c : c + 1, :].astype(F32), (16, Q))
    parts = split3(ldp_v[...])
    ccol_all = sum(dot_nt(tri, part) for part in parts)
    ccol_v[...] = ccol_all
    dt_all = dot_nt(eye, docm_v[...].astype(BF))
    c_end, d_end = ccol_all[Q - 1 : Q, :], dt_all[Q - 1 : Q, :]
    df = jnp.broadcast_to(docm_v[0:1, 0:1], (1, 128))
    dl = jnp.broadcast_to(docm_v[127:128, 127:128], (1, 128))
    end_parts = split3(jnp.broadcast_to(c_end, (8, 128)))
    before = ones(same_head & (sub // 16 < lane // 16))
    off = sum(dot(part, before) for part in end_parts)[0:1, :]
    total = sum(dot(part, ones(same_head)) for part in end_parts)[0:1, :]
    prev = jnp.where(head_lane < 16, df, pltpu.roll(d_end, 16, 1))
    w_exs = jnp.where(dt_all == dl, jnp.exp2(total - off - ccol_all), 0.0).astype(BF)

    def ag_got(unit):
        place = x_at((3, 3, 1, 1, 2, 2)[unit])
        ref = go_rows(place, core, unit % 2)
        remote(ref, ref, agx_s.at[unit], agx_r.at[unit], left).wait_recv()
        if unit == 0:
            send(ref, ref, agx_s.at[4], agx_r.at[4], right)
        if unit == 3:
            send(ref, ref, agx_s.at[5], agx_r.at[5], left)
        send(ref, ref, agd_s.at[unit], agd_r.at[unit], partner)

    def ag_pair_got(unit):
        place = x_at((3, 3, 1, 1, 2, 2)[unit])
        ref = go_rows(place, 1 - core, unit % 2)
        remote(ref, ref, agd_s.at[unit], agd_r.at[unit], partner).wait_recv()

    loads[0].wait()
    for c in range(CHUNKS):
        rows = slice(c * Q, (c + 1) * Q)
        exs = dot(w_exs * in_block(c), spread_v[...]).astype(BF)
        exs_v[rows, :] = exs
        dy_v[rows, :] = x_v[rows, :] * exs
    loads[1].wait()
    y1s[...] = dot_tn(wk[...], dy_v[...]).astype(BF)
    m1s[...] = stacked([total, df, dl], 8)
    own_q = pl.ds(pl.multiple_of(y * QR, QR), QR)
    m1r[y] = m1s[...]
    y1r[y] = y1s[own_q, :]
    for r in range(1, NY):
        q_rows = pl.ds(pl.multiple_of(((y + r) % NY) * QR, QR), QR)
        send(m1s, m1r.at[y], m1_ss.at[r], m1_rs.at[r], y_peer(r))
        send(y1s.at[q_rows, :], y1r.at[y], y1_ss.at[r], y1_rs.at[r], y_peer(r))

    skip_rows = [
        jnp.where(head_lane < HP, skip[2 * p], skip[2 * p + 1]) for p in range(PAIRS)
    ]

    def pair(p):
        return slice(p * 128, (p + 1) * 128)

    def doubled(v):
        return jnp.concatenate([v * m_lo, v * m_hi], axis=0)

    crow_v[...] = sum(dot_nt(part, tri) for part in parts)
    wexc_v[...] = jnp.where(dt_all == d_end, jnp.exp2(c_end - ccol_all), 0.0).astype(BF)
    wenc_v[...] = jnp.where(dt_all == prev, jnp.exp2(ccol_all), 0.0).astype(BF)
    wens_v[...] = jnp.where(dt_all == df, jnp.exp2(ccol_all + off), 0.0).astype(BF)
    block_decay = jnp.where(d_end == prev, jnp.exp2(c_end), 0.0)
    of_block = lax.broadcasted_iota(jnp.int32, (CHUNKS, 128), 0) == (
        lax.broadcasted_iota(jnp.int32, (CHUNKS, 128), 1) // 16
    )
    block_decay = jnp.where(of_block, block_decay, 0.0)
    coarse = block_decay.astype(BF)
    fine = (block_decay - coarse.astype(F32)).astype(BF)
    bd_v[...] = dot(coarse, spread_v[...]) + dot(fine, spread_v[...])
    run_v[...] = jnp.zeros_like(run_v)

    def inner_chunk(c):
        rows = rows_of(c)
        mine_only = in_block(c)
        exc = dot(wexc_v[...] * mine_only, spread_v[...]).astype(BF)
        exc_v[rows, :] = exc
        enc = dot(wenc_v[...] * mine_only, spread_v[...])
        enc_v[rows, :] = enc.astype(BF)
        ens_v[rows, :] = dot(wens_v[...] * mine_only, spread_v[...]).astype(BF)
        run = run_v[...]
        enter_v[c] = run.astype(BF)
        b, k = wk[rows, :], rk[rows, :]
        run_v[...] = run * bd_v[pl.ds(c, 1), :] + dot_tn(b, x_v[rows, :] * exc)
        ccol = pltpu.roll(ccol_v[...], (128 - 16 * c) % 128, 1)
        crow = crow_v[pl.ds(pl.multiple_of(c * 16, 16), 16), :]
        doc_row = docs[pl.ds(c, 1), :].astype(F32)
        dt = dot_nt(eye, jnp.broadcast_to(doc_row, (Q, Q)).astype(BF))
        same = dt == doc_row
        sm = jnp.where(same & (sub >= lane), dot_nt(k, b), 0.0)
        stm = jnp.where(same & (lane >= sub), dot_nt(b, k), 0.0)
        for p in range(PAIRS):
            ws, wts = [], []
            for h in (2 * p, 2 * p + 1):
                gap = ccol[:, h : h + 1] - crow[h : h + 1, :]
                ws.append((jnp.exp2(jnp.minimum(gap, 0.0)) * sm).astype(BF))
                wts.append((jnp.exp2(jnp.minimum(-gap, 0.0)) * stm).astype(BF))
            wt_v[c, p] = jnp.concatenate(wts, axis=1)
            xp = x_v[rows, pair(p)]
            mixed = dot(jnp.concatenate(ws, axis=1), doubled(xp))
            mixed += enc_v[rows, pair(p)].astype(F32) * dot(k, enter_v[c, :, pair(p)])
            mix_v[rows, pair(p)] = mixed + skip_rows[p] * xp.astype(F32)
            gate = g_v[rows, pair(p)].astype(F32)
            silu_v[rows, pair(p)] = gate / (1.0 + jnp.exp(-gate))

    loads[2].wait()
    loads[3].wait()
    pl.loop(0, 4)(inner_chunk)

    for r in range(1, NY):
        source = (y + NY - r) % NY
        remote(m1s, m1r.at[source], m1_ss.at[r], m1_rs.at[r], y_peer(r)).wait_recv()
        remote(y1s.at[own_q, :], y1r.at[source], y1_ss.at[r], y1_rs.at[r], y_peer(r)).wait_recv()
    meta = [m1r[j] for j in range(NY)]
    ls = [m[0:1, :] for m in meta]
    dfs = [m[1:2, :] for m in meta]
    dls = [m[2:3, :] for m in meta]

    def span(values):
        out = jnp.zeros((1, 128), F32)
        for v in values:
            out = out + v
        return out

    def gated_decay(a, b, values):
        return jnp.where(a == b, jnp.exp2(span(values)), 0.0)

    t_rows = [gated_decay(dls[j], dls[NY - 1], ls[j + 1 :]) for j in range(NY)]
    t_rows += [gated_decay(dfs[j], dfs[0], ls[:j]) for j in range(NY)]
    zrow_v[...] = expand_row(stacked(t_rows, 8))
    zs[...] = sum(zrow_v[j : j + 1, :] * y1r[j].astype(F32) for j in range(NY)).astype(BF)
    mzs[...] = stacked([span(ls), dfs[0], dls[NY - 1]], 8)
    zr[z] = zs[...]
    mzr[z] = mzs[...]
    for r in range(1, NZ):
        send(mzs, mzr.at[z], mz_ss.at[r], mz_rs.at[r], z_peer(r))
        send(zs, zr.at[z], z_ss.at[r], z_rs.at[r], z_peer(r))

    in_row = [(j, k) for k in range(NY) for j in range(k)]
    f_rows = [gated_decay(dls[j], dfs[k], ls[j + 1 : k]) for j, k in in_row]
    f_rows += [gated_decay(dfs[0], dfs[k], ls[:k]) for k in range(NY)]
    wrow_v[...] = expand_row(stacked(f_rows, 16))
    b_rows = [gated_decay(dfs[k], dls[j], ls[j + 1 : k]) for j, k in in_row]
    b_rows += [gated_decay(dls[NY - 1], dls[k], ls[k + 1 :]) for k in range(NY)]
    brow_v[...] = expand_row(stacked(b_rows, 16))

    ag_got(0)
    ag_got(3)

    pl.loop(4, CHUNKS)(inner_chunk)

    loads[4].wait()
    loads[5].wait()

    def grad_mix_of(place, first=False):
        rows = pl.ds(pl.multiple_of(place * 2 * Q, 2 * Q), 2 * Q)
        grad = dot_nt(go_v[rows, :], wo_v[...])
        dy = (grad * silu_v[rows, :]).astype(BF)
        dy_v[rows, :] = dy
        state = dot_tn(rk[rows, :], dy * ens_v[rows, :])
        gsum_v[...] = state if first else gsum_v[...] + state

    pair_own = go_v.at[pl.ds(pl.multiple_of((xx * 2 + 1 - core) * Q, Q), Q), :]
    remote(pair_own, pair_own, agd_s.at[6], agd_r.at[6], partner).wait_recv()
    grad_mix_of(xx, first=True)

    ag_got(1)
    ag_got(2)
    ag_pair_got(0)
    ag_pair_got(1)
    grad_mix_of(x_at(3))

    for r in range(1, NZ):
        source = (z + NZ - r) % NZ
        remote(mzs, mzr.at[source], mz_ss.at[r], mz_rs.at[r], z_peer(r)).wait_recv()
        remote(zs, zr.at[source], z_ss.at[r], z_rs.at[r], z_peer(r)).wait_recv()
    zmeta = [mzr[i] for i in range(NZ)]
    rls = [m[0:1, :] for m in zmeta]
    rdfs = [m[1:2, :] for m in zmeta]
    rdls = [m[2:3, :] for m in zmeta]

    def flag(condition):
        return jnp.where(condition, 1.0, 0.0).astype(F32)

    zf_rows, zb_rows = [], []
    for i in range(NZ):
        gap = span([rls[m] * flag(m < z) for m in range(i + 1, NZ)])
        zf_rows.append(flag(i < z) * jnp.where(rdls[i] == dfs[0], jnp.exp2(gap), 0.0))
        gap = span([rls[m] * flag(m > z) for m in range(i)])
        zb_rows.append(flag(i > z) * jnp.where(rdfs[i] == dls[NY - 1], jnp.exp2(gap), 0.0))
    zf = expand_row(stacked(zf_rows, 8))
    row_state = sum(zf[i : i + 1, :] * zr[i].astype(F32) for i in range(NZ))
    for k in range(NY):
        out = wrow_v[6 + k : 7 + k, :] * row_state
        for place, (j, kk) in enumerate(in_row):
            if kk == k:
                out += wrow_v[place : place + 1, :] * y1r[j].astype(F32)
        y2s[k * QR : (k + 1) * QR, :] = out.astype(BF)
    y2r[own_q, :] = y2s[own_q, :]
    for r in range(1, NY):
        q_rows = pl.ds(pl.multiple_of(((y + r) % NY) * QR, QR), QR)
        send(y2s.at[q_rows, :], y2r.at[own_q, :], y2_ss.at[r], y2_rs.at[r], y_peer(r))
    zrow_b = expand_row(stacked(zb_rows, 8))

    ag_pair_got(2)
    ag_pair_got(3)
    grad_mix_of(x_at(1))

    for r in range(1, NY):
        source = pl.ds(pl.multiple_of(((y + NY - r) % NY) * QR, QR), QR)
        remote(y2s.at[own_q, :], y2r.at[source, :], y2_ss.at[r], y2_rs.at[r], y_peer(r)).wait_recv()

    order = [x_at(2), x_at(1), x_at(3), xx]
    mine = pl.ds(pl.multiple_of(core * Q, Q), Q)
    theirs = pl.ds(pl.multiple_of((1 - core) * Q, Q), Q)

    def project(k):
        rows = pl.ds(pl.multiple_of(order[k] * 2 * Q, 2 * Q), 2 * Q)
        carried = ens_v[rows, :].astype(F32) * dot(rk[rows, :], y2r[...])
        gated = ((mix_v[rows, :] + carried) * silu_v[rows, :]).astype(BF)
        for n in range(5):
            cols = slice(n * 512, (n + 1) * 512)
            pall[k, :, cols] = dot(gated, wo_v[:, cols]).astype(BF)
        send(pall.at[k, theirs, :], pr.at[k], d_ss.at[k], d_rs.at[k], partner)

    def pair_sum(k, start, count):
        rows = pl.ds(pl.multiple_of(core * Q + start, HALF), count)
        return pall[k, rows, :].astype(F32) + pr[k, start : start + count, :].astype(F32)

    def pair_got(k):
        remote(pall.at[k, mine, :], pr.at[k], d_ss.at[k], d_rs.at[k], partner).wait_recv()

    def half(ref, which):
        return ref.at[pl.ds(which * HALF, HALF), :]

    project(0)
    project(1)
    pair_got(0)
    qs[0] = pair_sum(0, 0, Q).astype(BF)
    send(half(qs.at[0], 0), rla, rx_ss.at[0], rx_rs.at[0], right)
    send(half(qs.at[0], 1), rlb, rx_ss.at[1], rx_rs.at[1], left)

    ag_got(4)
    ag_got(5)
    ag_pair_got(4)
    ag_pair_got(5)
    grad_mix_of(x_at(2))
    b1s[...] = gsum_v[...].astype(BF)
    b1r[y] = b1s[own_q, :]
    for r in range(1, NY):
        q_rows = pl.ds(pl.multiple_of(((y + r) % NY) * QR, QR), QR)
        send(b1s.at[q_rows, :], b1r.at[y], b1_ss.at[r], b1_rs.at[r], y_peer(r))

    pair_got(1)
    qs[1, HALF:Q, :] = pair_sum(1, HALF, HALF).astype(BF)
    send(half(qs.at[1], 1), half(fl, 1), rx_ss.at[2], rx_rs.at[2], right)
    project(2)
    project(3)
    pair_got(2)
    qs[2, 0:HALF, :] = pair_sum(2, 0, HALF).astype(BF)
    send(half(qs.at[2], 0), half(fr, 0), rx_ss.at[3], rx_rs.at[3], left)

    def relay():
        remote(half(qs.at[0], 0), rla, rx_ss.at[0], rx_rs.at[0], right).wait_recv()
        qs[1, 0:HALF, :] = (pair_sum(1, 0, HALF) + rla[...].astype(F32)).astype(BF)
        send(half(qs.at[1], 0), half(fl, 0), rx_ss.at[4], rx_rs.at[4], right)
        remote(half(qs.at[0], 1), rlb, rx_ss.at[1], rx_rs.at[1], left).wait_recv()
        qs[2, HALF:Q, :] = (pair_sum(2, HALF, HALF) + rlb[...].astype(F32)).astype(BF)
        send(half(qs.at[2], 1), half(fr, 1), rx_ss.at[5], rx_rs.at[5], left)

    run_v[...] = jnp.zeros_like(run_v)

    def grad_chunk(back):
        c = CHUNKS - 1 - back
        rows = rows_of(c)
        b = wk[rows, :]
        run = run_v[...]
        run_v[...] = bd_v[pl.ds(c, 1), :] * run + dot_tn(rk[rows, :], dy_v[rows, :] * enc_v[rows, :])
        arr = run.astype(BF)
        arr_v[...] = arr
        for p in range(PAIRS):
            dyp = dy_v[rows, pair(p)]
            grad = dot(wt_v[c, p], doubled(dyp))
            grad += exc_v[rows, pair(p)].astype(F32) * dot(b, arr_v[:, pair(p)])
            gl_v[rows, pair(p)] = grad + skip_rows[p] * dyp.astype(F32)

    pl.loop(0, 4)(grad_chunk)

    for r in range(1, NY):
        source = (y + NY - r) % NY
        remote(b1s.at[own_q, :], b1r.at[source], b1_ss.at[r], b1_rs.at[r], y_peer(r)).wait_recv()
    bzs[...] = sum(
        zrow_v[NY + j : NY + j + 1, :] * b1r[j].astype(F32) for j in range(NY)
    ).astype(BF)
    bzr[z] = bzs[...]
    for r in range(1, NZ):
        send(bzs, bzr.at[z], bz_ss.at[r], bz_rs.at[r], z_peer(r))

    relay()
    pl.loop(4, CHUNKS)(grad_chunk)

    for r in range(1, NZ):
        source = (z + NZ - r) % NZ
        remote(bzs, bzr.at[source], bz_ss.at[r], bz_rs.at[r], z_peer(r)).wait_recv()
    row_state = sum(zrow_b[i : i + 1, :] * bzr[i].astype(F32) for i in range(NZ))
    for k in range(NY):
        out = brow_v[6 + k : 7 + k, :] * row_state
        for place, (kk, j) in enumerate(in_row):
            if kk == k:
                out += brow_v[place : place + 1, :] * b1r[j].astype(F32)
        b2s[k * QR : (k + 1) * QR, :] = out.astype(BF)
    b2r[own_q, :] = b2s[own_q, :]
    for r in range(1, NY):
        q_rows = pl.ds(pl.multiple_of(((y + r) % NY) * QR, QR), QR)
        send(b2s.at[q_rows, :], b2r.at[own_q, :], b2_ss.at[r], b2_rs.at[r], y_peer(r))

    pair_got(3)
    qs[3] = pair_sum(3, 0, Q).astype(BF)

    for r in range(1, NY):
        source = pl.ds(pl.multiple_of(((y + NY - r) % NY) * QR, QR), QR)
        remote(b2s.at[own_q, :], b2r.at[source, :], b2_ss.at[r], b2_rs.at[r], y_peer(r)).wait_recv()

    @pl.loop(0, CHUNKS // 2)
    def _(k):
        rows = pl.ds(pl.multiple_of(k * 2 * Q, 2 * Q), 2 * Q)
        carried = exs_v[rows, :].astype(F32) * dot(wk[rows, :], b2r[...])
        gi[rows, :] = (gl_v[rows, :] + carried).astype(BF)

    remote(half(qs.at[1], 1), half(fl, 1), rx_ss.at[2], rx_rs.at[2], right).wait_recv()
    remote(half(qs.at[2], 0), half(fr, 0), rx_ss.at[3], rx_rs.at[3], left).wait_recv()
    remote(half(qs.at[1], 0), half(fl, 0), rx_ss.at[4], rx_rs.at[4], right).wait_recv()
    remote(half(qs.at[2], 1), half(fr, 1), rx_ss.at[5], rx_rs.at[5], left).wait_recv()
    mo[...] = (qs[3].astype(F32) + fl[...].astype(F32) + fr[...].astype(F32)).astype(BF)

    for copy in started:
        copy.wait_send()


def write_out(mo, gi, mo_out, gi_out, sem):
    copies = [
        pltpu.make_async_copy(mo, mo_out, sem.at[0]),
        pltpu.make_async_copy(gi, gi_out, sem.at[1]),
    ]
    for copy in copies:
        copy.start()
    for copy in copies:
        copy.wait()


def shards(
    inputs, gates, write_keys, read_keys, log_decay, skip_gain, doc_ids, out_weight, grad_out
):
    vmem = pl.BlockSpec(memory_space=pltpu.VMEM)
    smem = pl.BlockSpec(memory_space=pltpu.SMEM)
    hbm = pl.BlockSpec(memory_space=pl.ANY)
    v = lambda shape, kind=BF: pltpu.VMEM(shape, kind)
    dma = lambda *shape: pltpu.SemaphoreType.DMA(shape)
    full, square = (TOK, WIDTH), (128, 128)
    scratch = [
        v(full), v(full), v((TOK, N)), v((TOK, N)), v((WIDTH, D)), v((TOK, D)),
        v(full, F32), v(full, F32), v(full, F32),
        v(full), v(full), v(full), v(full), v((CHUNKS, PAIRS, Q, 2 * Q)), v(full),
        v((CHUNKS, N, WIDTH)), v((N, WIDTH)), v((N, WIDTH), F32),
        v((N, WIDTH), F32), v(square, F32), v(square, F32), v(square, F32), v(square, F32),
        v(square), v(square), v(square), v((CHUNKS, WIDTH), F32),
        v((128, WIDTH)),
        v((N, WIDTH)), v((NY, QR, WIDTH)), v((8, 128), F32), v((NY, 8, 128), F32),
        v((QR, WIDTH)), v((NZ, QR, WIDTH)), v((8, 128), F32), v((NZ, 8, 128), F32),
        v((N, WIDTH)), v((N, WIDTH)), v((16, WIDTH), F32), v((16, WIDTH), F32),
        v((8, WIDTH), F32),
        v((N, WIDTH)), v((NY, QR, WIDTH)), v((QR, WIDTH)), v((NZ, QR, WIDTH)),
        v((N, WIDTH)), v((N, WIDTH)),
        v((NX, 2 * Q, D)), v((NX, Q, D)), v((NX, Q, D)), v((HALF, D)), v((HALF, D)),
        v((Q, D)), v((Q, D)),
        dma(6), dma(6), dma(6), dma(7), dma(7),
        dma(NY), dma(NY), dma(NY), dma(NY), dma(NZ), dma(NZ), dma(NZ), dma(NZ), dma(NY), dma(NY),
        dma(NY), dma(NY), dma(NZ), dma(NZ), dma(NY), dma(NY),
        dma(4), dma(4), dma(6), dma(6),
    ]
    results = pl.pallas_call(
        kernel,
        out_shape=(pltpu.VMEM((Q, D), BF), pltpu.VMEM((TOK, WIDTH), BF)),
        in_specs=[hbm, hbm, hbm, hbm, vmem, smem, vmem, hbm, hbm],
        out_specs=(vmem, vmem),
        scratch_shapes=scratch,
        compiler_params=pltpu.CompilerParams(
            collective_id=0, has_side_effects=True, vmem_limit_bytes=54 * 1024 * 1024
        ),
    )(
        inputs, gates, write_keys, read_keys, log_decay, skip_gain,
        doc_ids.reshape(CHUNKS, Q), out_weight, grad_out,
    )
    return pl.pallas_call(
        write_out,
        out_shape=(
            jax.ShapeDtypeStruct((Q, D), BF),
            jax.ShapeDtypeStruct((TOK, WIDTH), BF),
        ),
        in_specs=[vmem, vmem],
        out_specs=(hbm, hbm),
        scratch_shapes=[dma(2)],
        compiler_params=pltpu.CompilerParams(vmem_limit_bytes=1024 * 1024),
    )(*results)


def solution(mesh):
    return jax.shard_map(
        shards,
        mesh=mesh,
        in_specs=(
            P("seq", "head"),
            P("seq", "head"),
            P("seq", None),
            P("seq", None),
            P("head", "seq"),
            P("head"),
            P("seq"),
            P("head", None),
            P(("seq", "head"), None),
        ),
        out_specs=(P(("seq", "head"), None), P("seq", "head")),
        check_vma=False,
    )
```

```python
import math

import jax
import jax.numpy as jnp
from jax import lax
from jax.experimental import pallas as pl
from jax.experimental.pallas import tpu as pltpu
from jax.sharding import PartitionSpec as P

NX, NY, NZ = 4, 4, 8
Y_STEPS, Z_STEPS = (2, 1, 3), (4, 3, 5, 2, 6, 1, 7)
Q = 128
CHUNKS = 8
TOK = Q * CHUNKS
HEADS = 10
PAIRS = 5
HP = 64
WIDTH = HEADS * HP
N = 128
D = 2560
QR = N // NY
HALF = 64
LOG2E = 1.0 / math.log(2.0)
MESH = pl.DeviceIdType.MESH
BF = jnp.bfloat16
F32 = jnp.float32


def dot(a, b):
    return jnp.dot(a, b, preferred_element_type=F32)


def dot_nt(a, b):
    return lax.dot_general(a, b, (((1,), (1,)), ((), ())), preferred_element_type=F32)


def dot_tn(a, b):
    return lax.dot_general(a, b, (((0,), (0,)), ((), ())), preferred_element_type=F32)


def split3(v):
    a = v.astype(BF)
    rest = v - a.astype(F32)
    b = rest.astype(BF)
    return a, b, (rest - b.astype(F32)).astype(BF)


def stacked(rows, count):
    place = lax.broadcasted_iota(jnp.int32, (count, 128), 0)
    out = jnp.zeros((count, 128), F32)
    for k, row in enumerate(rows):
        out = jnp.where(place == k, row, out)
    return out


def kernel(
    x_hbm, g_hbm, wk_hbm, rk_hbm, ld, skip, docs, wo_hbm, go_hbm,
    mo, gi,
    x_v, g_v, wk, rk, wo_v, go_v, silu_v, mix_v, gl_v, exc_v, enc_v, exs_v, ens_v, wt_v, dy_v,
    enter_v, arr_v, gsum_v, run_v, ldp_v, docm_v, ccol_v, crow_v, wexc_v, wenc_v, wens_v, bd_v,
    spread_v,
    y1s, y1r, m1s, m1r, zs, zr, mzs, mzr, y2s, y2r, wrow_v, brow_v, zrow_v, zf_v, zb_v,
    b1s, b1r, bzs, bzr, b2s, b2r,
    pall, pr, qs, rla, rlb, fl, fr,
    lsem, agx_s, agx_r, agd_s, agd_r,
    y1_ss, y1_rs, m1_ss, m1_rs, z_ss, z_rs, mz_ss, mz_rs, y2_ss, y2_rs,
    b1_ss, b1_rs, bz_ss, bz_rs, b2_ss, b2_rs,
    d_ss, d_rs, rx_ss, rx_rs,
):
    seq = lax.axis_index("seq")
    head = lax.axis_index("head")
    z, y = seq // NY, seq % NY
    xx, core = head // 2, head % 2
    x_at = lambda k: (xx + k) % NX

    def dev(seq_id, head_id):
        return {"seq": seq_id, "head": head_id}

    right = dev(seq, x_at(1) * 2 + core)
    left = dev(seq, x_at(3) * 2 + core)
    partner = dev(seq, xx * 2 + 1 - core)
    y_peer = lambda r: dev(z * NY + (y + r) % NY, head)
    z_peer = lambda r: dev(((z + r) % NZ) * NY + y, head)

    def remote(src, dst, ss, rs, to):
        return pltpu.make_async_remote_copy(
            src_ref=src, dst_ref=dst, send_sem=ss, recv_sem=rs, device_id=to, device_id_type=MESH
        )

    started = []

    def send(*args):
        copy = remote(*args)
        copy.start()
        started.append(copy)

    own_rows = pl.ds(pl.multiple_of(head * Q, Q), Q)
    loads = [
        pltpu.make_async_copy(x_hbm, x_v, lsem.at[0]),
        pltpu.make_async_copy(wk_hbm, wk, lsem.at[1]),
        pltpu.make_async_copy(rk_hbm, rk, lsem.at[2]),
        pltpu.make_async_copy(g_hbm, g_v, lsem.at[3]),
        pltpu.make_async_copy(go_hbm, go_v.at[own_rows, :], lsem.at[4]),
        pltpu.make_async_copy(wo_hbm, wo_v, lsem.at[5]),
    ]

    barrier = pltpu.get_barrier_semaphore()
    peers = [right, left, partner]
    peers += [y_peer(r) for r in Y_STEPS] + [z_peer(r) for r in Z_STEPS]
    for peer in peers:
        pl.semaphore_signal(barrier, inc=1, device_id=peer, device_id_type=MESH)
    for copy in loads:
        copy.start()
    pl.semaphore_wait(barrier, len(peers))

    def go_rows(place, of_core, half):
        start = pl.multiple_of((place * 2 + of_core) * Q + half * HALF, HALF)
        return go_v.at[pl.ds(start, HALF), :]

    for half in (0, 1):
        part = go_hbm.at[pl.ds(half * HALF, HALF), :]
        send(part, go_rows(xx, core, half), agx_s.at[half], agx_r.at[half], right)
        part = go_hbm.at[pl.ds((1 - half) * HALF, HALF), :]
        send(part, go_rows(xx, core, 1 - half), agx_s.at[3 - half], agx_r.at[3 - half], left)
    send(go_hbm, go_v.at[own_rows, :], agd_s.at[6], agd_r.at[6], partner)

    sub = lax.broadcasted_iota(jnp.int32, (Q, Q), 0)
    lane = lax.broadcasted_iota(jnp.int32, (Q, Q), 1)
    ones = lambda condition: condition.astype(F32).astype(BF)
    tri = ones(lane <= sub)
    eye = ones(lane == sub)
    head_lane = lax.broadcasted_iota(jnp.int32, (1, 128), 1)
    same_head = (sub % 16) == (lane % 16)
    head_of = lax.broadcasted_iota(jnp.int32, (128, WIDTH), 1) // HP
    spread_v[...] = ones(head_of == lax.broadcasted_iota(jnp.int32, (128, WIDTH), 0) % 16)
    m_lo = ones(head_lane < HP)
    m_hi = ones(head_lane >= HP)

    def in_block(c):
        return ones(head_lane // 16 == c)

    def expand_row(w):
        w = jnp.where(head_lane < 16, w, 0.0)
        a = w.astype(BF)
        return dot(a, spread_v[...]) + dot((w - a.astype(F32)).astype(BF), spread_v[...])

    def rows_of(c):
        return pl.ds(pl.multiple_of(c * Q, Q), Q)

    ldp_v[...] = jnp.zeros_like(ldp_v)
    for c in range(CHUNKS):
        ldp_v[16 * c : 16 * c + HEADS, :] = ld[:, c * Q : (c + 1) * Q] * LOG2E
        docm_v[16 * c : 16 * c + 16, :] = jnp.broadcast_to(docs[c : c + 1, :].astype(F32), (16, Q))
    parts = split3(ldp_v[...])
    ccol_all = sum(dot_nt(tri, part) for part in parts)
    ccol_v[...] = ccol_all
    dt_all = dot_nt(eye, docm_v[...].astype(BF))
    c_end, d_end = ccol_all[Q - 1 : Q, :], dt_all[Q - 1 : Q, :]
    df = jnp.broadcast_to(docm_v[0:1, 0:1], (1, 128))
    dl = jnp.broadcast_to(docm_v[127:128, 127:128], (1, 128))
    end_parts = split3(jnp.broadcast_to(c_end, (8, 128)))
    before = ones(same_head & (sub // 16 < lane // 16))
    off = sum(dot(part, before) for part in end_parts)[0:1, :]
    total = sum(dot(part, ones(same_head)) for part in end_parts)[0:1, :]
    prev = jnp.where(head_lane < 16, df, pltpu.roll(d_end, 16, 1))
    w_exs = jnp.where(dt_all == dl, jnp.exp2(total - off - ccol_all), 0.0).astype(BF)

    def ag_got(unit):
        place = x_at((3, 3, 1, 1, 2, 2)[unit])
        ref = go_rows(place, core, unit % 2)
        remote(ref, ref, agx_s.at[unit], agx_r.at[unit], left).wait_recv()
        if unit == 0:
            send(ref, ref, agx_s.at[4], agx_r.at[4], right)
        if unit == 3:
            send(ref, ref, agx_s.at[5], agx_r.at[5], left)
        send(ref, ref, agd_s.at[unit], agd_r.at[unit], partner)

    def ag_pair_got(unit):
        place = x_at((3, 3, 1, 1, 2, 2)[unit])
        ref = go_rows(place, 1 - core, unit % 2)
        remote(ref, ref, agd_s.at[unit], agd_r.at[unit], partner).wait_recv()

    m1s[...] = stacked([total, df, dl], 8)
    m1r[y] = m1s[...]
    for r in Y_STEPS:
        send(m1s, m1r.at[y], m1_ss.at[r], m1_rs.at[r], y_peer(r))

    loads[0].wait()
    for c in range(CHUNKS):
        rows = slice(c * Q, (c + 1) * Q)
        exs = dot(w_exs * in_block(c), spread_v[...]).astype(BF)
        exs_v[rows, :] = exs
        dy_v[rows, :] = x_v[rows, :] * exs
    loads[1].wait()
    y1s[...] = dot_tn(wk[...], dy_v[...]).astype(BF)
    own_q = pl.ds(pl.multiple_of(y * QR, QR), QR)
    y1r[y] = y1s[own_q, :]
    for r in Y_STEPS:
        q_rows = pl.ds(pl.multiple_of(((y + r) % NY) * QR, QR), QR)
        send(y1s.at[q_rows, :], y1r.at[y], y1_ss.at[r], y1_rs.at[r], y_peer(r))

    skip_rows = [
        jnp.where(head_lane < HP, skip[2 * p], skip[2 * p + 1]) for p in range(PAIRS)
    ]

    def pair(p):
        return slice(p * 128, (p + 1) * 128)

    def doubled(v):
        return jnp.concatenate([v * m_lo, v * m_hi], axis=0)

    crow_v[...] = sum(dot_nt(part, tri) for part in parts)
    wexc_v[...] = jnp.where(dt_all == d_end, jnp.exp2(c_end - ccol_all), 0.0).astype(BF)
    wenc_v[...] = jnp.where(dt_all == prev, jnp.exp2(ccol_all), 0.0).astype(BF)
    wens_v[...] = jnp.where(dt_all == df, jnp.exp2(ccol_all + off), 0.0).astype(BF)
    block_decay = jnp.where(d_end == prev, jnp.exp2(c_end), 0.0)
    of_block = lax.broadcasted_iota(jnp.int32, (CHUNKS, 128), 0) == (
        lax.broadcasted_iota(jnp.int32, (CHUNKS, 128), 1) // 16
    )
    block_decay = jnp.where(of_block, block_decay, 0.0)
    coarse = block_decay.astype(BF)
    fine = (block_decay - coarse.astype(F32)).astype(BF)
    bd_v[...] = dot(coarse, spread_v[...]) + dot(fine, spread_v[...])
    run_v[...] = jnp.zeros_like(run_v)

    def inner_chunk(c):
        rows = rows_of(c)
        mine_only = in_block(c)
        exc = dot(wexc_v[...] * mine_only, spread_v[...]).astype(BF)
        exc_v[rows, :] = exc
        enc = dot(wenc_v[...] * mine_only, spread_v[...])
        enc_v[rows, :] = enc.astype(BF)
        ens_v[rows, :] = dot(wens_v[...] * mine_only, spread_v[...]).astype(BF)
        run = run_v[...]
        enter_v[c] = run.astype(BF)
        b, k = wk[rows, :], rk[rows, :]
        run_v[...] = run * bd_v[pl.ds(c, 1), :] + dot_tn(b, x_v[rows, :] * exc)
        ccol = pltpu.roll(ccol_v[...], (128 - 16 * c) % 128, 1)
        crow = crow_v[pl.ds(pl.multiple_of(c * 16, 16), 16), :]
        doc_row = docs[pl.ds(c, 1), :].astype(F32)
        dt = dot_nt(eye, jnp.broadcast_to(doc_row, (Q, Q)).astype(BF))
        same = dt == doc_row
        sm = jnp.where(same & (sub >= lane), dot_nt(k, b), 0.0)
        stm = jnp.where(same & (lane >= sub), dot_nt(b, k), 0.0)
        for p in range(PAIRS):
            ws, wts = [], []
            for h in (2 * p, 2 * p + 1):
                gap = ccol[:, h : h + 1] - crow[h : h + 1, :]
                ws.append((jnp.exp2(jnp.minimum(gap, 0.0)) * sm).astype(BF))
                wts.append((jnp.exp2(jnp.minimum(-gap, 0.0)) * stm).astype(BF))
            wt_v[c, p] = jnp.concatenate(wts, axis=1)
            xp = x_v[rows, pair(p)]
            mixed = dot(jnp.concatenate(ws, axis=1), doubled(xp))
            mixed += enc_v[rows, pair(p)].astype(F32) * dot(k, enter_v[c, :, pair(p)])
            mix_v[rows, pair(p)] = mixed + skip_rows[p] * xp.astype(F32)
            gate = g_v[rows, pair(p)].astype(F32)
            silu_v[rows, pair(p)] = gate / (1.0 + jnp.exp(-gate))

    loads[2].wait()
    loads[3].wait()
    pl.loop(0, 2)(inner_chunk)

    for r in Y_STEPS:
        source = (y + NY - r) % NY
        remote(m1s, m1r.at[source], m1_ss.at[r], m1_rs.at[r], y_peer(r)).wait_recv()
    meta = [m1r[j] for j in range(NY)]
    ls = [m[0:1, :] for m in meta]
    dfs = [m[1:2, :] for m in meta]
    dls = [m[2:3, :] for m in meta]

    def span(values):
        out = jnp.zeros((1, 128), F32)
        for v in values:
            out = out + v
        return out

    def gated_decay(a, b, values):
        return jnp.where(a == b, jnp.exp2(span(values)), 0.0)

    mzs[...] = stacked([span(ls), dfs[0], dls[NY - 1]], 8)
    mzr[z] = mzs[...]
    for r in Z_STEPS:
        send(mzs, mzr.at[z], mz_ss.at[r], mz_rs.at[r], z_peer(r))
    t_rows = [gated_decay(dls[j], dls[NY - 1], ls[j + 1 :]) for j in range(NY)]
    t_rows += [gated_decay(dfs[j], dfs[0], ls[:j]) for j in range(NY)]
    zrow_v[...] = expand_row(stacked(t_rows, 8))
    in_row = [(j, k) for k in range(NY) for j in range(k)]
    f_rows = [gated_decay(dls[j], dfs[k], ls[j + 1 : k]) for j, k in in_row]
    f_rows += [gated_decay(dfs[0], dfs[k], ls[:k]) for k in range(NY)]
    wrow_v[...] = expand_row(stacked(f_rows, 16))
    b_rows = [gated_decay(dfs[k], dls[j], ls[j + 1 : k]) for j, k in in_row]
    b_rows += [gated_decay(dls[NY - 1], dls[k], ls[k + 1 :]) for k in range(NY)]
    brow_v[...] = expand_row(stacked(b_rows, 16))

    pl.loop(2, 4)(inner_chunk)

    for r in Y_STEPS:
        source = (y + NY - r) % NY
        remote(y1s.at[own_q, :], y1r.at[source], y1_ss.at[r], y1_rs.at[r], y_peer(r)).wait_recv()
    zs[...] = sum(zrow_v[j : j + 1, :] * y1r[j].astype(F32) for j in range(NY)).astype(BF)
    zr[z] = zs[...]
    for r in Z_STEPS:
        send(zs, zr.at[z], z_ss.at[r], z_rs.at[r], z_peer(r))

    ag_got(0)
    ag_got(3)

    pl.loop(4, CHUNKS)(inner_chunk)

    loads[4].wait()
    loads[5].wait()

    def grad_mix_of(place, first=False):
        rows = pl.ds(pl.multiple_of(place * 2 * Q, 2 * Q), 2 * Q)
        grad = dot_nt(go_v[rows, :], wo_v[...])
        dy = (grad * silu_v[rows, :]).astype(BF)
        dy_v[rows, :] = dy
        state = dot_tn(rk[rows, :], dy * ens_v[rows, :])
        gsum_v[...] = state if first else gsum_v[...] + state

    pair_own = go_v.at[pl.ds(pl.multiple_of((xx * 2 + 1 - core) * Q, Q), Q), :]
    remote(pair_own, pair_own, agd_s.at[6], agd_r.at[6], partner).wait_recv()
    grad_mix_of(xx, first=True)

    for r in Z_STEPS:
        source = (z + NZ - r) % NZ
        remote(mzs, mzr.at[source], mz_ss.at[r], mz_rs.at[r], z_peer(r)).wait_recv()
    zmeta = [mzr[i] for i in range(NZ)]
    rls = [m[0:1, :] for m in zmeta]
    rdfs = [m[1:2, :] for m in zmeta]
    rdls = [m[2:3, :] for m in zmeta]

    def flag(condition):
        return jnp.where(condition, 1.0, 0.0).astype(F32)

    zf_rows, zb_rows = [], []
    for i in range(NZ):
        gap = span([rls[m] * flag(m < z) for m in range(i + 1, NZ)])
        zf_rows.append(flag(i < z) * jnp.where(rdls[i] == dfs[0], jnp.exp2(gap), 0.0))
        gap = span([rls[m] * flag(m > z) for m in range(i)])
        zb_rows.append(flag(i > z) * jnp.where(rdfs[i] == dls[NY - 1], jnp.exp2(gap), 0.0))
    zf_v[...] = expand_row(stacked(zf_rows, 8))
    zb_v[...] = expand_row(stacked(zb_rows, 8))

    ag_got(1)
    ag_got(2)

    for r in Z_STEPS:
        source = (z + NZ - r) % NZ
        remote(zs, zr.at[source], z_ss.at[r], z_rs.at[r], z_peer(r)).wait_recv()
    row_state = sum(zf_v[i : i + 1, :] * zr[i].astype(F32) for i in range(NZ))
    for k in range(NY):
        out = wrow_v[6 + k : 7 + k, :] * row_state
        for place, (j, kk) in enumerate(in_row):
            if kk == k:
                out += wrow_v[place : place + 1, :] * y1r[j].astype(F32)
        y2s[k * QR : (k + 1) * QR, :] = out.astype(BF)
    y2r[own_q, :] = y2s[own_q, :]
    for r in Y_STEPS:
        q_rows = pl.ds(pl.multiple_of(((y + r) % NY) * QR, QR), QR)
        send(y2s.at[q_rows, :], y2r.at[own_q, :], y2_ss.at[r], y2_rs.at[r], y_peer(r))

    ag_pair_got(0)
    ag_pair_got(1)
    grad_mix_of(x_at(3))
    ag_pair_got(2)
    ag_pair_got(3)
    grad_mix_of(x_at(1))

    for r in Y_STEPS:
        source = pl.ds(pl.multiple_of(((y + NY - r) % NY) * QR, QR), QR)
        remote(y2s.at[own_q, :], y2r.at[source, :], y2_ss.at[r], y2_rs.at[r], y_peer(r)).wait_recv()

    order = [x_at(2), x_at(1), x_at(3), xx]
    mine = pl.ds(pl.multiple_of(core * Q, Q), Q)
    theirs = pl.ds(pl.multiple_of((1 - core) * Q, Q), Q)

    def project_rows(k, start, count):
        rows = pl.ds(pl.multiple_of(order[k] * 2 * Q + start, Q), count)
        to_rows = pl.ds(pl.multiple_of(start, Q), count)
        carried = ens_v[rows, :].astype(F32) * dot(rk[rows, :], y2r[...])
        gated = ((mix_v[rows, :] + carried) * silu_v[rows, :]).astype(BF)
        for n in range(5):
            cols = slice(n * 512, (n + 1) * 512)
            pall[k, to_rows, cols] = dot(gated, wo_v[:, cols]).astype(BF)

    def to_partner(k):
        send(pall.at[k, theirs, :], pr.at[k], d_ss.at[k], d_rs.at[k], partner)

    def project(k):
        project_rows(k, 0, 2 * Q)
        to_partner(k)

    def pair_sum(k, start, count):
        rows = pl.ds(pl.multiple_of(core * Q + start, HALF), count)
        return pall[k, rows, :].astype(F32) + pr[k, start : start + count, :].astype(F32)

    def pair_got(k):
        remote(pall.at[k, mine, :], pr.at[k], d_ss.at[k], d_rs.at[k], partner).wait_recv()

    def half(ref, which):
        return ref.at[pl.ds(which * HALF, HALF), :]

    project_rows(0, (1 - core) * Q, Q)
    to_partner(0)
    project_rows(0, core * Q, Q)
    ag_got(4)
    ag_got(5)
    pair_got(0)
    qs[0] = pair_sum(0, 0, Q).astype(BF)
    send(half(qs.at[0], 0), rla, rx_ss.at[0], rx_rs.at[0], right)
    send(half(qs.at[0], 1), rlb, rx_ss.at[1], rx_rs.at[1], left)
    project(1)

    ag_pair_got(4)
    ag_pair_got(5)
    grad_mix_of(x_at(2))
    b1s[...] = gsum_v[...].astype(BF)
    b1r[y] = b1s[own_q, :]
    for r in Y_STEPS:
        q_rows = pl.ds(pl.multiple_of(((y + r) % NY) * QR, QR), QR)
        send(b1s.at[q_rows, :], b1r.at[y], b1_ss.at[r], b1_rs.at[r], y_peer(r))

    pair_got(1)
    qs[1, HALF:Q, :] = pair_sum(1, HALF, HALF).astype(BF)
    send(half(qs.at[1], 1), half(fl, 1), rx_ss.at[2], rx_rs.at[2], right)
    project(2)
    project(3)
    pair_got(2)
    qs[2, 0:HALF, :] = pair_sum(2, 0, HALF).astype(BF)
    send(half(qs.at[2], 0), half(fr, 0), rx_ss.at[3], rx_rs.at[3], left)

    def relay():
        remote(half(qs.at[0], 0), rla, rx_ss.at[0], rx_rs.at[0], right).wait_recv()
        qs[1, 0:HALF, :] = (pair_sum(1, 0, HALF) + rla[...].astype(F32)).astype(BF)
        send(half(qs.at[1], 0), half(fl, 0), rx_ss.at[4], rx_rs.at[4], right)
        remote(half(qs.at[0], 1), rlb, rx_ss.at[1], rx_rs.at[1], left).wait_recv()
        qs[2, HALF:Q, :] = (pair_sum(2, HALF, HALF) + rlb[...].astype(F32)).astype(BF)
        send(half(qs.at[2], 1), half(fr, 1), rx_ss.at[5], rx_rs.at[5], left)

    run_v[...] = jnp.zeros_like(run_v)

    def grad_chunk(back):
        c = CHUNKS - 1 - back
        rows = rows_of(c)
        b = wk[rows, :]
        run = run_v[...]
        run_v[...] = bd_v[pl.ds(c, 1), :] * run + dot_tn(rk[rows, :], dy_v[rows, :] * enc_v[rows, :])
        arr = run.astype(BF)
        arr_v[...] = arr
        for p in range(PAIRS):
            dyp = dy_v[rows, pair(p)]
            grad = dot(wt_v[c, p], doubled(dyp))
            grad += exc_v[rows, pair(p)].astype(F32) * dot(b, arr_v[:, pair(p)])
            gl_v[rows, pair(p)] = grad + skip_rows[p] * dyp.astype(F32)

    pl.loop(0, 4)(grad_chunk)

    for r in Y_STEPS:
        source = (y + NY - r) % NY
        remote(b1s.at[own_q, :], b1r.at[source], b1_ss.at[r], b1_rs.at[r], y_peer(r)).wait_recv()
    bzs[...] = sum(
        zrow_v[NY + j : NY + j + 1, :] * b1r[j].astype(F32) for j in range(NY)
    ).astype(BF)
    bzr[z] = bzs[...]
    for r in Z_STEPS:
        send(bzs, bzr.at[z], bz_ss.at[r], bz_rs.at[r], z_peer(r))

    relay()
    pl.loop(4, CHUNKS)(grad_chunk)

    for r in Z_STEPS:
        source = (z + NZ - r) % NZ
        remote(bzs, bzr.at[source], bz_ss.at[r], bz_rs.at[r], z_peer(r)).wait_recv()
    row_state = sum(zb_v[i : i + 1, :] * bzr[i].astype(F32) for i in range(NZ))
    for k in range(NY):
        out = brow_v[6 + k : 7 + k, :] * row_state
        for place, (kk, j) in enumerate(in_row):
            if kk == k:
                out += brow_v[place : place + 1, :] * b1r[j].astype(F32)
        b2s[k * QR : (k + 1) * QR, :] = out.astype(BF)
    b2r[own_q, :] = b2s[own_q, :]
    for r in Y_STEPS:
        q_rows = pl.ds(pl.multiple_of(((y + r) % NY) * QR, QR), QR)
        send(b2s.at[q_rows, :], b2r.at[own_q, :], b2_ss.at[r], b2_rs.at[r], y_peer(r))

    pair_got(3)
    qs[3] = pair_sum(3, 0, Q).astype(BF)

    for r in Y_STEPS:
        source = pl.ds(pl.multiple_of(((y + NY - r) % NY) * QR, QR), QR)
        remote(b2s.at[own_q, :], b2r.at[source, :], b2_ss.at[r], b2_rs.at[r], y_peer(r)).wait_recv()

    @pl.loop(0, CHUNKS // 2)
    def _(k):
        rows = pl.ds(pl.multiple_of(k * 2 * Q, 2 * Q), 2 * Q)
        carried = exs_v[rows, :].astype(F32) * dot(wk[rows, :], b2r[...])
        gi[rows, :] = (gl_v[rows, :] + carried).astype(BF)

    remote(half(qs.at[1], 1), half(fl, 1), rx_ss.at[2], rx_rs.at[2], right).wait_recv()
    remote(half(qs.at[2], 0), half(fr, 0), rx_ss.at[3], rx_rs.at[3], left).wait_recv()
    remote(half(qs.at[1], 0), half(fl, 0), rx_ss.at[4], rx_rs.at[4], right).wait_recv()
    remote(half(qs.at[2], 1), half(fr, 1), rx_ss.at[5], rx_rs.at[5], left).wait_recv()
    mo[...] = (qs[3].astype(F32) + fl[...].astype(F32) + fr[...].astype(F32)).astype(BF)

    for copy in started:
        copy.wait_send()


def write_out(mo, gi, mo_out, gi_out, sem):
    copies = [
        pltpu.make_async_copy(mo, mo_out, sem.at[0]),
        pltpu.make_async_copy(gi, gi_out, sem.at[1]),
    ]
    for copy in copies:
        copy.start()
    for copy in copies:
        copy.wait()


def shards(
    inputs, gates, write_keys, read_keys, log_decay, skip_gain, doc_ids, out_weight, grad_out
):
    vmem = pl.BlockSpec(memory_space=pltpu.VMEM)
    smem = pl.BlockSpec(memory_space=pltpu.SMEM)
    hbm = pl.BlockSpec(memory_space=pl.ANY)
    v = lambda shape, kind=BF: pltpu.VMEM(shape, kind)
    dma = lambda *shape: pltpu.SemaphoreType.DMA(shape)
    full, square = (TOK, WIDTH), (128, 128)
    scratch = [
        v(full), v(full), v((TOK, N)), v((TOK, N)), v((WIDTH, D)), v((TOK, D)),
        v(full, F32), v(full, F32), v(full, F32),
        v(full), v(full), v(full), v(full), v((CHUNKS, PAIRS, Q, 2 * Q)), v(full),
        v((CHUNKS, N, WIDTH)), v((N, WIDTH)), v((N, WIDTH), F32),
        v((N, WIDTH), F32), v(square, F32), v(square, F32), v(square, F32), v(square, F32),
        v(square), v(square), v(square), v((CHUNKS, WIDTH), F32),
        v((128, WIDTH)),
        v((N, WIDTH)), v((NY, QR, WIDTH)), v((8, 128), F32), v((NY, 8, 128), F32),
        v((QR, WIDTH)), v((NZ, QR, WIDTH)), v((8, 128), F32), v((NZ, 8, 128), F32),
        v((N, WIDTH)), v((N, WIDTH)), v((16, WIDTH), F32), v((16, WIDTH), F32),
        v((8, WIDTH), F32), v((8, WIDTH), F32), v((8, WIDTH), F32),
        v((N, WIDTH)), v((NY, QR, WIDTH)), v((QR, WIDTH)), v((NZ, QR, WIDTH)),
        v((N, WIDTH)), v((N, WIDTH)),
        v((NX, 2 * Q, D)), v((NX, Q, D)), v((NX, Q, D)), v((HALF, D)), v((HALF, D)),
        v((Q, D)), v((Q, D)),
        dma(6), dma(6), dma(6), dma(7), dma(7),
        dma(NY), dma(NY), dma(NY), dma(NY), dma(NZ), dma(NZ), dma(NZ), dma(NZ), dma(NY), dma(NY),
        dma(NY), dma(NY), dma(NZ), dma(NZ), dma(NY), dma(NY),
        dma(4), dma(4), dma(6), dma(6),
    ]
    results = pl.pallas_call(
        kernel,
        out_shape=(pltpu.VMEM((Q, D), BF), pltpu.VMEM((TOK, WIDTH), BF)),
        in_specs=[hbm, hbm, hbm, hbm, vmem, smem, vmem, hbm, hbm],
        out_specs=(vmem, vmem),
        scratch_shapes=scratch,
        compiler_params=pltpu.CompilerParams(
            collective_id=0, has_side_effects=True, vmem_limit_bytes=54 * 1024 * 1024
        ),
    )(
        inputs, gates, write_keys, read_keys, log_decay, skip_gain,
        doc_ids.reshape(CHUNKS, Q), out_weight, grad_out,
    )
    return pl.pallas_call(
        write_out,
        out_shape=(
            jax.ShapeDtypeStruct((Q, D), BF),
            jax.ShapeDtypeStruct((TOK, WIDTH), BF),
        ),
        in_specs=[vmem, vmem],
        out_specs=(hbm, hbm),
        scratch_shapes=[dma(2)],
        compiler_params=pltpu.CompilerParams(vmem_limit_bytes=1024 * 1024),
    )(*results)


def solution(mesh):
    return jax.shard_map(
        shards,
        mesh=mesh,
        in_specs=(
            P("seq", "head"),
            P("seq", "head"),
            P("seq", None),
            P("seq", None),
            P("head", "seq"),
            P("head"),
            P("seq"),
            P("head", None),
            P(("seq", "head"), None),
        ),
        out_specs=(P(("seq", "head"), None), P("seq", "head")),
        check_vma=False,
    )
```

```python
import math

import jax
import jax.numpy as jnp
from jax import lax
from jax.experimental import pallas as pl
from jax.experimental.pallas import tpu as pltpu
from jax.sharding import PartitionSpec as P

NX, NY, NZ = 4, 4, 8
Y_STEPS, Z_STEPS = (2, 1, 3), (4, 3, 5, 2, 6, 1, 7)
Q = 128
CHUNKS = 8
TOK = Q * CHUNKS
HEADS = 10
PAIRS = 5
HP = 64
WIDTH = HEADS * HP
N = 128
D = 2560
QR = N // NY
HALF = 64
LOG2E = 1.0 / math.log(2.0)
MESH = pl.DeviceIdType.MESH
BF = jnp.bfloat16
F32 = jnp.float32


def dot(a, b):
    return jnp.dot(a, b, preferred_element_type=F32)


def dot_nt(a, b):
    return lax.dot_general(a, b, (((1,), (1,)), ((), ())), preferred_element_type=F32)


def dot_tn(a, b):
    return lax.dot_general(a, b, (((0,), (0,)), ((), ())), preferred_element_type=F32)


def split3(v):
    a = v.astype(BF)
    rest = v - a.astype(F32)
    b = rest.astype(BF)
    return a, b, (rest - b.astype(F32)).astype(BF)


def stacked(rows, count):
    place = lax.broadcasted_iota(jnp.int32, (count, 128), 0)
    out = jnp.zeros((count, 128), F32)
    for k, row in enumerate(rows):
        out = jnp.where(place == k, row, out)
    return out


def kernel(
    x_hbm, g_hbm, wk_hbm, rk_hbm, ld, skip, docs, wo_hbm, go_hbm,
    mo, gi,
    x_v, g_v, wk, rk, wo_v, go_v, silu_v, mix_v, gl_v, exc_v, enc_v, exs_v, ens_v, wt_v, dy_v,
    enter_v, arr_v, gsum_v, run_v, ldp_v, docm_v, ccol_v, crow_v, wexc_v, wenc_v, wens_v, bd_v,
    spread_v,
    y1s, y1r, m1s, m1r, zs, zr, mzs, mzr, y2s, y2r, wrow_v, brow_v, zrow_v, zf_v, zb_v,
    b1s, b1r, bzs, bzr, b2s, b2r,
    pall, pr, qs, rla, rlb, fl, fr,
    lsem, agx_s, agx_r, agd_s, agd_r,
    y1_ss, y1_rs, m1_ss, m1_rs, z_ss, z_rs, mz_ss, mz_rs, y2_ss, y2_rs,
    b1_ss, b1_rs, bz_ss, bz_rs, b2_ss, b2_rs,
    d_ss, d_rs, rx_ss, rx_rs,
):
    seq = lax.axis_index("seq")
    head = lax.axis_index("head")
    z, y = seq // NY, seq % NY
    xx, core = head // 2, head % 2
    x_at = lambda k: (xx + k) % NX

    def dev(seq_id, head_id):
        return {"seq": seq_id, "head": head_id}

    right = dev(seq, x_at(1) * 2 + core)
    left = dev(seq, x_at(3) * 2 + core)
    partner = dev(seq, xx * 2 + 1 - core)
    y_peer = lambda r: dev(z * NY + (y + r) % NY, head)
    z_peer = lambda r: dev(((z + r) % NZ) * NY + y, head)

    def remote(src, dst, ss, rs, to):
        return pltpu.make_async_remote_copy(
            src_ref=src, dst_ref=dst, send_sem=ss, recv_sem=rs, device_id=to, device_id_type=MESH
        )

    started = []

    def send(*args):
        copy = remote(*args)
        copy.start()
        started.append(copy)

    sent_where = []

    def send_where(condition, *args):
        copy = remote(*args)
        pl.when(condition)(copy.start)
        sent_where.append((condition, copy))

    own_rows = pl.ds(pl.multiple_of(head * Q, Q), Q)
    loads = [
        pltpu.make_async_copy(x_hbm, x_v, lsem.at[0]),
        pltpu.make_async_copy(wk_hbm, wk, lsem.at[1]),
        pltpu.make_async_copy(rk_hbm, rk, lsem.at[2]),
        pltpu.make_async_copy(g_hbm, g_v, lsem.at[3]),
        pltpu.make_async_copy(go_hbm, go_v.at[own_rows, :], lsem.at[4]),
        pltpu.make_async_copy(wo_hbm, wo_v, lsem.at[5]),
    ]

    zr[...] = jnp.zeros_like(zr)
    bzr[...] = jnp.zeros_like(bzr)
    barrier = pltpu.get_barrier_semaphore()
    peers = [right, left, partner]
    peers += [y_peer(r) for r in Y_STEPS] + [z_peer(r) for r in Z_STEPS]
    for peer in peers:
        pl.semaphore_signal(barrier, inc=1, device_id=peer, device_id_type=MESH)
    for copy in loads:
        copy.start()
    pl.semaphore_wait(barrier, len(peers))

    def go_rows(place, of_core, half):
        start = pl.multiple_of((place * 2 + of_core) * Q + half * HALF, HALF)
        return go_v.at[pl.ds(start, HALF), :]

    for half in (0, 1):
        part = go_hbm.at[pl.ds(half * HALF, HALF), :]
        send(part, go_rows(xx, core, half), agx_s.at[half], agx_r.at[half], right)
        part = go_hbm.at[pl.ds((1 - half) * HALF, HALF), :]
        send(part, go_rows(xx, core, 1 - half), agx_s.at[3 - half], agx_r.at[3 - half], left)
    send(go_hbm, go_v.at[own_rows, :], agd_s.at[8], agd_r.at[8], partner)

    sub = lax.broadcasted_iota(jnp.int32, (Q, Q), 0)
    lane = lax.broadcasted_iota(jnp.int32, (Q, Q), 1)
    ones = lambda condition: condition.astype(F32).astype(BF)
    tri = ones(lane <= sub)
    eye = ones(lane == sub)
    head_lane = lax.broadcasted_iota(jnp.int32, (1, 128), 1)
    same_head = (sub % 16) == (lane % 16)
    head_of = lax.broadcasted_iota(jnp.int32, (128, WIDTH), 1) // HP
    spread_v[...] = ones(head_of == lax.broadcasted_iota(jnp.int32, (128, WIDTH), 0) % 16)
    m_lo = ones(head_lane < HP)
    m_hi = ones(head_lane >= HP)

    def in_block(c):
        return ones(head_lane // 16 == c)

    def expand_row(w):
        w = jnp.where(head_lane < 16, w, 0.0)
        a = w.astype(BF)
        return dot(a, spread_v[...]) + dot((w - a.astype(F32)).astype(BF), spread_v[...])

    def rows_of(c):
        return pl.ds(pl.multiple_of(c * Q, Q), Q)

    ldp_v[...] = jnp.zeros_like(ldp_v)
    for c in range(CHUNKS):
        ldp_v[16 * c : 16 * c + HEADS, :] = ld[:, c * Q : (c + 1) * Q] * LOG2E
        docm_v[16 * c : 16 * c + 16, :] = jnp.broadcast_to(docs[c : c + 1, :].astype(F32), (16, Q))
    parts = split3(ldp_v[...])
    ccol_all = sum(dot_nt(tri, part) for part in parts)
    ccol_v[...] = ccol_all
    dt_all = dot_nt(eye, docm_v[...].astype(BF))
    c_end, d_end = ccol_all[Q - 1 : Q, :], dt_all[Q - 1 : Q, :]
    df = jnp.broadcast_to(docm_v[0:1, 0:1], (1, 128))
    dl = jnp.broadcast_to(docm_v[127:128, 127:128], (1, 128))
    end_parts = split3(jnp.broadcast_to(c_end, (8, 128)))
    before = ones(same_head & (sub // 16 < lane // 16))
    off = sum(dot(part, before) for part in end_parts)[0:1, :]
    total = sum(dot(part, ones(same_head)) for part in end_parts)[0:1, :]
    prev = jnp.where(head_lane < 16, df, pltpu.roll(d_end, 16, 1))
    w_exs = jnp.where(dt_all == dl, jnp.exp2(total - off - ccol_all), 0.0).astype(BF)

    def ag_rows(unit, of_core):
        if unit < 4:
            return go_rows(x_at((3, 3, 1, 1)[unit]), of_core, unit % 2)
        start = (x_at(2) * 2 + of_core) * Q + (unit - 4) * (HALF // 2)
        return go_v.at[pl.ds(pl.multiple_of(start, HALF // 2), HALF // 2), :]

    def ag_got(unit):
        ref = ag_rows(unit, core)
        remote(ref, ref, agx_s.at[unit], agx_r.at[unit], left).wait_recv()
        if unit in (0, 3):
            place, to = (x_at(3), right) if unit == 0 else (x_at(1), left)
            for piece in (0, 1):
                start = (place * 2 + core) * Q + (unit % 2) * HALF + piece * (HALF // 2)
                rows = pl.ds(pl.multiple_of(start, HALF // 2), HALF // 2)
                far = 4 + (unit % 2) * 2 + piece
                send(go_v.at[rows, :], go_v.at[rows, :], agx_s.at[far], agx_r.at[far], to)
        send(ref, ref, agd_s.at[unit], agd_r.at[unit], partner)

    def ag_pair_got(unit):
        ref = ag_rows(unit, 1 - core)
        remote(ref, ref, agd_s.at[unit], agd_r.at[unit], partner).wait_recv()

    m1s[...] = stacked([total, df, dl], 8)
    m1r[y] = m1s[...]
    for r in Y_STEPS:
        send(m1s, m1r.at[y], m1_ss.at[r], m1_rs.at[r], y_peer(r))

    loads[0].wait()
    for c in range(CHUNKS):
        rows = slice(c * Q, (c + 1) * Q)
        exs = dot(w_exs * in_block(c), spread_v[...]).astype(BF)
        exs_v[rows, :] = exs
        dy_v[rows, :] = x_v[rows, :] * exs
    loads[1].wait()
    y1s[...] = dot_tn(wk[...], dy_v[...]).astype(BF)
    own_q = pl.ds(pl.multiple_of(y * QR, QR), QR)
    y1r[y] = y1s[own_q, :]
    for r in Y_STEPS:
        q_rows = pl.ds(pl.multiple_of(((y + r) % NY) * QR, QR), QR)
        send(y1s.at[q_rows, :], y1r.at[y], y1_ss.at[r], y1_rs.at[r], y_peer(r))

    skip_rows = [
        jnp.where(head_lane < HP, skip[2 * p], skip[2 * p + 1]) for p in range(PAIRS)
    ]

    def pair(p):
        return slice(p * 128, (p + 1) * 128)

    def doubled(v):
        return jnp.concatenate([v * m_lo, v * m_hi], axis=0)

    crow_v[...] = sum(dot_nt(part, tri) for part in parts)
    wexc_v[...] = jnp.where(dt_all == d_end, jnp.exp2(c_end - ccol_all), 0.0).astype(BF)
    wenc_v[...] = jnp.where(dt_all == prev, jnp.exp2(ccol_all), 0.0).astype(BF)
    wens_v[...] = jnp.where(dt_all == df, jnp.exp2(ccol_all + off), 0.0).astype(BF)
    block_decay = jnp.where(d_end == prev, jnp.exp2(c_end), 0.0)
    of_block = lax.broadcasted_iota(jnp.int32, (CHUNKS, 128), 0) == (
        lax.broadcasted_iota(jnp.int32, (CHUNKS, 128), 1) // 16
    )
    block_decay = jnp.where(of_block, block_decay, 0.0)
    coarse = block_decay.astype(BF)
    fine = (block_decay - coarse.astype(F32)).astype(BF)
    bd_v[...] = dot(coarse, spread_v[...]) + dot(fine, spread_v[...])
    run_v[...] = jnp.zeros_like(run_v)

    def inner_chunk(c):
        rows = rows_of(c)
        mine_only = in_block(c)
        exc = dot(wexc_v[...] * mine_only, spread_v[...]).astype(BF)
        exc_v[rows, :] = exc
        enc = dot(wenc_v[...] * mine_only, spread_v[...])
        enc_v[rows, :] = enc.astype(BF)
        ens_v[rows, :] = dot(wens_v[...] * mine_only, spread_v[...]).astype(BF)
        run = run_v[...]
        enter_v[c] = run.astype(BF)
        b, k = wk[rows, :], rk[rows, :]
        run_v[...] = run * bd_v[pl.ds(c, 1), :] + dot_tn(b, x_v[rows, :] * exc)
        ccol = pltpu.roll(ccol_v[...], (128 - 16 * c) % 128, 1)
        crow = crow_v[pl.ds(pl.multiple_of(c * 16, 16), 16), :]
        doc_row = docs[pl.ds(c, 1), :].astype(F32)
        dt = dot_nt(eye, jnp.broadcast_to(doc_row, (Q, Q)).astype(BF))
        same = dt == doc_row
        sm = jnp.where(same & (sub >= lane), dot_nt(k, b), 0.0)
        stm = jnp.where(same & (lane >= sub), dot_nt(b, k), 0.0)
        for p in range(PAIRS):
            ws, wts = [], []
            for h in (2 * p, 2 * p + 1):
                gap = ccol[:, h : h + 1] - crow[h : h + 1, :]
                ws.append((jnp.exp2(jnp.minimum(gap, 0.0)) * sm).astype(BF))
                wts.append((jnp.exp2(jnp.minimum(-gap, 0.0)) * stm).astype(BF))
            wt_v[c, p] = jnp.concatenate(wts, axis=1)
            xp = x_v[rows, pair(p)]
            mixed = dot(jnp.concatenate(ws, axis=1), doubled(xp))
            mixed += enc_v[rows, pair(p)].astype(F32) * dot(k, enter_v[c, :, pair(p)])
            mix_v[rows, pair(p)] = mixed + skip_rows[p] * xp.astype(F32)
            gate = g_v[rows, pair(p)].astype(F32)
            silu_v[rows, pair(p)] = gate / (1.0 + jnp.exp(-gate))

    loads[2].wait()
    loads[3].wait()
    pl.loop(0, 2)(inner_chunk)

    for r in Y_STEPS:
        source = (y + NY - r) % NY
        remote(m1s, m1r.at[source], m1_ss.at[r], m1_rs.at[r], y_peer(r)).wait_recv()
    meta = [m1r[j] for j in range(NY)]
    ls = [m[0:1, :] for m in meta]
    dfs = [m[1:2, :] for m in meta]
    dls = [m[2:3, :] for m in meta]

    def span(values):
        out = jnp.zeros((1, 128), F32)
        for v in values:
            out = out + v
        return out

    def gated_decay(a, b, values):
        return jnp.where(a == b, jnp.exp2(span(values)), 0.0)

    mzs[...] = stacked([span(ls), dfs[0], dls[NY - 1]], 8)
    mzr[z] = mzs[...]
    for r in Z_STEPS:
        send(mzs, mzr.at[z], mz_ss.at[r], mz_rs.at[r], z_peer(r))
    t_rows = [gated_decay(dls[j], dls[NY - 1], ls[j + 1 :]) for j in range(NY)]
    t_rows += [gated_decay(dfs[j], dfs[0], ls[:j]) for j in range(NY)]
    zrow_v[...] = expand_row(stacked(t_rows, 8))
    in_row = [(j, k) for k in range(NY) for j in range(k)]
    f_rows = [gated_decay(dls[j], dfs[k], ls[j + 1 : k]) for j, k in in_row]
    f_rows += [gated_decay(dfs[0], dfs[k], ls[:k]) for k in range(NY)]
    wrow_v[...] = expand_row(stacked(f_rows, 16))
    b_rows = [gated_decay(dfs[k], dls[j], ls[j + 1 : k]) for j, k in in_row]
    b_rows += [gated_decay(dls[NY - 1], dls[k], ls[k + 1 :]) for k in range(NY)]
    brow_v[...] = expand_row(stacked(b_rows, 16))

    pl.loop(2, 4)(inner_chunk)

    for r in Y_STEPS:
        source = (y + NY - r) % NY
        remote(y1s.at[own_q, :], y1r.at[source], y1_ss.at[r], y1_rs.at[r], y_peer(r)).wait_recv()
    zs[...] = sum(zrow_v[j : j + 1, :] * y1r[j].astype(F32) for j in range(NY)).astype(BF)
    zr[z] = zs[...]
    for r in Z_STEPS:
        send_where(z + r < NZ, zs, zr.at[z], z_ss.at[r], z_rs.at[r], z_peer(r))

    ag_got(0)
    ag_got(3)

    pl.loop(4, CHUNKS)(inner_chunk)

    loads[4].wait()
    loads[5].wait()

    def grad_mix_rows(start, count, first=False):
        rows = pl.ds(pl.multiple_of(start, Q), count)
        grad = dot_nt(go_v[rows, :], wo_v[...])
        dy = (grad * silu_v[rows, :]).astype(BF)
        dy_v[rows, :] = dy
        state = dot_tn(rk[rows, :], dy * ens_v[rows, :])
        gsum_v[...] = state if first else gsum_v[...] + state

    def grad_mix_of(place, first=False):
        grad_mix_rows(place * 2 * Q, 2 * Q, first)

    pair_own = go_v.at[pl.ds(pl.multiple_of((xx * 2 + 1 - core) * Q, Q), Q), :]
    remote(pair_own, pair_own, agd_s.at[8], agd_r.at[8], partner).wait_recv()
    grad_mix_of(xx, first=True)

    for r in Z_STEPS:
        source = (z + NZ - r) % NZ
        remote(mzs, mzr.at[source], mz_ss.at[r], mz_rs.at[r], z_peer(r)).wait_recv()
    zmeta = [mzr[i] for i in range(NZ)]
    rls = [m[0:1, :] for m in zmeta]
    rdfs = [m[1:2, :] for m in zmeta]
    rdls = [m[2:3, :] for m in zmeta]

    def flag(condition):
        return jnp.where(condition, 1.0, 0.0).astype(F32)

    zf_rows, zb_rows = [], []
    for i in range(NZ):
        gap = span([rls[m] * flag(m < z) for m in range(i + 1, NZ)])
        zf_rows.append(flag(i < z) * jnp.where(rdls[i] == dfs[0], jnp.exp2(gap), 0.0))
        gap = span([rls[m] * flag(m > z) for m in range(i)])
        zb_rows.append(flag(i > z) * jnp.where(rdfs[i] == dls[NY - 1], jnp.exp2(gap), 0.0))
    zf_v[...] = expand_row(stacked(zf_rows, 8))
    zb_v[...] = expand_row(stacked(zb_rows, 8))

    ag_got(1)
    ag_got(2)

    for r in Z_STEPS:
        source = (z + NZ - r) % NZ
        total_of = remote(zs, zr.at[source], z_ss.at[r], z_rs.at[r], z_peer(r))
        pl.when(z >= r)(total_of.wait_recv)
    row_state = sum(zf_v[i : i + 1, :] * zr[i].astype(F32) for i in range(NZ))
    for k in range(NY):
        out = wrow_v[6 + k : 7 + k, :] * row_state
        for place, (j, kk) in enumerate(in_row):
            if kk == k:
                out += wrow_v[place : place + 1, :] * y1r[j].astype(F32)
        y2s[k * QR : (k + 1) * QR, :] = out.astype(BF)
    y2r[own_q, :] = y2s[own_q, :]
    for r in Y_STEPS:
        q_rows = pl.ds(pl.multiple_of(((y + r) % NY) * QR, QR), QR)
        send(y2s.at[q_rows, :], y2r.at[own_q, :], y2_ss.at[r], y2_rs.at[r], y_peer(r))

    ag_pair_got(0)
    ag_pair_got(1)
    grad_mix_of(x_at(3))
    ag_pair_got(2)
    ag_pair_got(3)
    grad_mix_of(x_at(1))

    for r in Y_STEPS:
        source = pl.ds(pl.multiple_of(((y + NY - r) % NY) * QR, QR), QR)
        remote(y2s.at[own_q, :], y2r.at[source, :], y2_ss.at[r], y2_rs.at[r], y_peer(r)).wait_recv()

    order = [x_at(2), x_at(1), x_at(3), xx]

    def project_rows(k, start, count):
        rows = pl.ds(pl.multiple_of(order[k] * 2 * Q + start, Q), count)
        to_rows = pl.ds(pl.multiple_of(start, Q), count)
        carried = ens_v[rows, :].astype(F32) * dot(rk[rows, :], y2r[...])
        gated = ((mix_v[rows, :] + carried) * silu_v[rows, :]).astype(BF)
        for n in range(5):
            cols = slice(n * 512, (n + 1) * 512)
            pall[k, to_rows, cols] = dot(gated, wo_v[:, cols]).astype(BF)

    def pair_copy(k, half, of_core):
        rows = pl.ds(pl.multiple_of(of_core * Q + half * HALF, HALF), HALF)
        to_rows = pl.ds(half * HALF, HALF)
        place = 2 * k + half
        return pall.at[k, rows, :], pr.at[k, to_rows, :], d_ss.at[place], d_rs.at[place], partner

    def to_partner(k, halves):
        for half in halves:
            send(*pair_copy(k, half, 1 - core))

    def project(k, halves):
        project_rows(k, 0, 2 * Q)
        to_partner(k, halves)

    def pair_sum(k, start, count):
        rows = pl.ds(pl.multiple_of(core * Q + start, HALF), count)
        return pall[k, rows, :].astype(F32) + pr[k, start : start + count, :].astype(F32)

    def pair_got(k, half):
        remote(*pair_copy(k, half, core)).wait_recv()

    def half(ref, which):
        return ref.at[pl.ds(which * HALF, HALF), :]

    project_rows(0, (1 - core) * Q, Q)
    to_partner(0, (0, 1))
    project_rows(0, core * Q, Q)
    for unit in (4, 6, 5, 7):
        ag_got(unit)
    for which, to, landing in ((0, right, rla), (1, left, rlb)):
        pair_got(0, which)
        rows = slice(which * HALF, (which + 1) * HALF)
        qs[0, rows, :] = pair_sum(0, which * HALF, HALF).astype(BF)
        send(half(qs.at[0], which), landing, rx_ss.at[which], rx_rs.at[which], to)

    grad_mix_rows((x_at(2) * 2 + core) * Q, Q)
    for unit in (4, 6, 5, 7):
        ag_pair_got(unit)
    grad_mix_rows((x_at(2) * 2 + 1 - core) * Q, Q)
    b1s[...] = gsum_v[...].astype(BF)
    b1r[y] = b1s[own_q, :]
    for r in Y_STEPS:
        q_rows = pl.ds(pl.multiple_of(((y + r) % NY) * QR, QR), QR)
        send(b1s.at[q_rows, :], b1r.at[y], b1_ss.at[r], b1_rs.at[r], y_peer(r))

    project(1, (1, 0))
    project(2, (0, 1))
    pair_got(1, 1)
    qs[1, HALF:Q, :] = pair_sum(1, HALF, HALF).astype(BF)
    send(half(qs.at[1], 1), half(fl, 1), rx_ss.at[2], rx_rs.at[2], right)
    pair_got(2, 0)
    qs[2, 0:HALF, :] = pair_sum(2, 0, HALF).astype(BF)
    send(half(qs.at[2], 0), half(fr, 0), rx_ss.at[3], rx_rs.at[3], left)
    project(3, (0, 1))

    def relay():
        remote(half(qs.at[0], 0), rla, rx_ss.at[0], rx_rs.at[0], right).wait_recv()
        pair_got(1, 0)
        qs[1, 0:HALF, :] = (pair_sum(1, 0, HALF) + rla[...].astype(F32)).astype(BF)
        send(half(qs.at[1], 0), half(fl, 0), rx_ss.at[4], rx_rs.at[4], right)
        remote(half(qs.at[0], 1), rlb, rx_ss.at[1], rx_rs.at[1], left).wait_recv()
        pair_got(2, 1)
        qs[2, HALF:Q, :] = (pair_sum(2, HALF, HALF) + rlb[...].astype(F32)).astype(BF)
        send(half(qs.at[2], 1), half(fr, 1), rx_ss.at[5], rx_rs.at[5], left)

    run_v[...] = jnp.zeros_like(run_v)

    def grad_chunk(back):
        c = CHUNKS - 1 - back
        rows = rows_of(c)
        b = wk[rows, :]
        run = run_v[...]
        run_v[...] = bd_v[pl.ds(c, 1), :] * run + dot_tn(rk[rows, :], dy_v[rows, :] * enc_v[rows, :])
        arr = run.astype(BF)
        arr_v[...] = arr
        for p in range(PAIRS):
            dyp = dy_v[rows, pair(p)]
            grad = dot(wt_v[c, p], doubled(dyp))
            grad += exc_v[rows, pair(p)].astype(F32) * dot(b, arr_v[:, pair(p)])
            gl_v[rows, pair(p)] = grad + skip_rows[p] * dyp.astype(F32)

    pl.loop(0, 4)(grad_chunk)

    for r in Y_STEPS:
        source = (y + NY - r) % NY
        remote(b1s.at[own_q, :], b1r.at[source], b1_ss.at[r], b1_rs.at[r], y_peer(r)).wait_recv()
    bzs[...] = sum(
        zrow_v[NY + j : NY + j + 1, :] * b1r[j].astype(F32) for j in range(NY)
    ).astype(BF)
    bzr[z] = bzs[...]
    for r in Z_STEPS:
        send_where(z + r >= NZ, bzs, bzr.at[z], bz_ss.at[r], bz_rs.at[r], z_peer(r))

    relay()
    pl.loop(4, CHUNKS)(grad_chunk)

    for r in Z_STEPS:
        source = (z + NZ - r) % NZ
        total_of = remote(bzs, bzr.at[source], bz_ss.at[r], bz_rs.at[r], z_peer(r))
        pl.when(z < r)(total_of.wait_recv)
    row_state = sum(zb_v[i : i + 1, :] * bzr[i].astype(F32) for i in range(NZ))
    for k in range(NY):
        out = brow_v[6 + k : 7 + k, :] * row_state
        for place, (kk, j) in enumerate(in_row):
            if kk == k:
                out += brow_v[place : place + 1, :] * b1r[j].astype(F32)
        b2s[k * QR : (k + 1) * QR, :] = out.astype(BF)
    b2r[own_q, :] = b2s[own_q, :]
    for r in Y_STEPS:
        q_rows = pl.ds(pl.multiple_of(((y + r) % NY) * QR, QR), QR)
        send(b2s.at[q_rows, :], b2r.at[own_q, :], b2_ss.at[r], b2_rs.at[r], y_peer(r))

    pair_got(3, 0)
    pair_got(3, 1)
    qs[3] = pair_sum(3, 0, Q).astype(BF)

    for r in Y_STEPS:
        source = pl.ds(pl.multiple_of(((y + NY - r) % NY) * QR, QR), QR)
        remote(b2s.at[own_q, :], b2r.at[source, :], b2_ss.at[r], b2_rs.at[r], y_peer(r)).wait_recv()

    @pl.loop(0, CHUNKS // 2)
    def _(k):
        rows = pl.ds(pl.multiple_of(k * 2 * Q, 2 * Q), 2 * Q)
        carried = exs_v[rows, :].astype(F32) * dot(wk[rows, :], b2r[...])
        gi[rows, :] = (gl_v[rows, :] + carried).astype(BF)

    remote(half(qs.at[1], 1), half(fl, 1), rx_ss.at[2], rx_rs.at[2], right).wait_recv()
    remote(half(qs.at[2], 0), half(fr, 0), rx_ss.at[3], rx_rs.at[3], left).wait_recv()
    remote(half(qs.at[1], 0), half(fl, 0), rx_ss.at[4], rx_rs.at[4], right).wait_recv()
    remote(half(qs.at[2], 1), half(fr, 1), rx_ss.at[5], rx_rs.at[5], left).wait_recv()
    mo[...] = (qs[3].astype(F32) + fl[...].astype(F32) + fr[...].astype(F32)).astype(BF)

    for copy in started:
        copy.wait_send()
    for condition, copy in sent_where:
        pl.when(condition)(copy.wait_send)


def write_out(mo, gi, mo_out, gi_out, sem):
    copies = []
    for ref, out in ((mo, mo_out), (gi, gi_out)):
        count = ref.shape[0] // 4
        for k in range(4):
            rows = pl.ds(k * count, count)
            place = sem.at[len(copies)]
            copies.append(pltpu.make_async_copy(ref.at[rows, :], out.at[rows, :], place))
    for copy in copies:
        copy.start()
    for copy in copies:
        copy.wait()


def shards(
    inputs, gates, write_keys, read_keys, log_decay, skip_gain, doc_ids, out_weight, grad_out
):
    vmem = pl.BlockSpec(memory_space=pltpu.VMEM)
    smem = pl.BlockSpec(memory_space=pltpu.SMEM)
    hbm = pl.BlockSpec(memory_space=pl.ANY)
    v = lambda shape, kind=BF: pltpu.VMEM(shape, kind)
    dma = lambda *shape: pltpu.SemaphoreType.DMA(shape)
    full, square = (TOK, WIDTH), (128, 128)
    scratch = [
        v(full), v(full), v((TOK, N)), v((TOK, N)), v((WIDTH, D)), v((TOK, D)),
        v(full, F32), v(full, F32), v(full, F32),
        v(full), v(full), v(full), v(full), v((CHUNKS, PAIRS, Q, 2 * Q)), v(full),
        v((CHUNKS, N, WIDTH)), v((N, WIDTH)), v((N, WIDTH), F32),
        v((N, WIDTH), F32), v(square, F32), v(square, F32), v(square, F32), v(square, F32),
        v(square), v(square), v(square), v((CHUNKS, WIDTH), F32),
        v((128, WIDTH)),
        v((N, WIDTH)), v((NY, QR, WIDTH)), v((8, 128), F32), v((NY, 8, 128), F32),
        v((QR, WIDTH)), v((NZ, QR, WIDTH)), v((8, 128), F32), v((NZ, 8, 128), F32),
        v((N, WIDTH)), v((N, WIDTH)), v((16, WIDTH), F32), v((16, WIDTH), F32),
        v((8, WIDTH), F32), v((8, WIDTH), F32), v((8, WIDTH), F32),
        v((N, WIDTH)), v((NY, QR, WIDTH)), v((QR, WIDTH)), v((NZ, QR, WIDTH)),
        v((N, WIDTH)), v((N, WIDTH)),
        v((NX, 2 * Q, D)), v((NX, Q, D)), v((NX, Q, D)), v((HALF, D)), v((HALF, D)),
        v((Q, D)), v((Q, D)),
        dma(6), dma(8), dma(8), dma(9), dma(9),
        dma(NY), dma(NY), dma(NY), dma(NY), dma(NZ), dma(NZ), dma(NZ), dma(NZ), dma(NY), dma(NY),
        dma(NY), dma(NY), dma(NZ), dma(NZ), dma(NY), dma(NY),
        dma(8), dma(8), dma(6), dma(6),
    ]
    results = pl.pallas_call(
        kernel,
        out_shape=(pltpu.VMEM((Q, D), BF), pltpu.VMEM((TOK, WIDTH), BF)),
        in_specs=[hbm, hbm, hbm, hbm, vmem, smem, vmem, hbm, hbm],
        out_specs=(vmem, vmem),
        scratch_shapes=scratch,
        compiler_params=pltpu.CompilerParams(
            collective_id=0, has_side_effects=True, vmem_limit_bytes=54 * 1024 * 1024
        ),
    )(
        inputs, gates, write_keys, read_keys, log_decay, skip_gain,
        doc_ids.reshape(CHUNKS, Q), out_weight, grad_out,
    )
    return pl.pallas_call(
        write_out,
        out_shape=(
            jax.ShapeDtypeStruct((Q, D), BF),
            jax.ShapeDtypeStruct((TOK, WIDTH), BF),
        ),
        in_specs=[vmem, vmem],
        out_specs=(hbm, hbm),
        scratch_shapes=[dma(8)],
        compiler_params=pltpu.CompilerParams(vmem_limit_bytes=1024 * 1024),
    )(*results)


def solution(mesh):
    return jax.shard_map(
        shards,
        mesh=mesh,
        in_specs=(
            P("seq", "head"),
            P("seq", "head"),
            P("seq", None),
            P("seq", None),
            P("head", "seq"),
            P("head"),
            P("seq"),
            P("head", None),
            P(("seq", "head"), None),
        ),
        out_specs=(P(("seq", "head"), None), P("seq", "head")),
        check_vma=False,
    )
```

```python
import math

import jax
import jax.numpy as jnp
from jax import lax
from jax.experimental import pallas as pl
from jax.experimental.pallas import tpu as pltpu
from jax.sharding import PartitionSpec as P

NX, NY, NZ = 4, 4, 8
Y_STEPS, Z_STEPS = (2, 1, 3), (4, 3, 5, 2, 6, 1, 7)
Q = 128
CHUNKS = 8
TOK = Q * CHUNKS
HEADS = 10
PAIRS = 5
HP = 64
WIDTH = HEADS * HP
N = 128
D = 2560
QR = N // NY
HALF = 64
LOG2E = 1.0 / math.log(2.0)
MESH = pl.DeviceIdType.MESH
BF = jnp.bfloat16
F32 = jnp.float32


def dot(a, b):
    return jnp.dot(a, b, preferred_element_type=F32)


def dot_nt(a, b):
    return lax.dot_general(a, b, (((1,), (1,)), ((), ())), preferred_element_type=F32)


def dot_tn(a, b):
    return lax.dot_general(a, b, (((0,), (0,)), ((), ())), preferred_element_type=F32)


def split3(v):
    a = v.astype(BF)
    rest = v - a.astype(F32)
    b = rest.astype(BF)
    return a, b, (rest - b.astype(F32)).astype(BF)


def stacked(rows, count):
    place = lax.broadcasted_iota(jnp.int32, (count, 128), 0)
    out = jnp.zeros((count, 128), F32)
    for k, row in enumerate(rows):
        out = jnp.where(place == k, row, out)
    return out


def kernel(
    x_hbm, g_hbm, wk_hbm, rk_hbm, ld, skip, docs, wo_hbm, go_hbm,
    mo, gi,
    x_v, g_v, wk, rk, wo_v, go_v, silu_v, mix_v, gl_v, exc_v, enc_v, exs_v, ens_v, wt_v, dy_v,
    enter_v, arr_v, gsum_v, run_v, ldp_v, docm_v, ccol_v, crow_v, wexc_v, wenc_v, wens_v, bd_v,
    spread_v,
    y1s, y1r, m1s, m1r, zs, zr, mzs, mzr, y2s, y2r, wrow_v, brow_v, zrow_v, zf_v, zb_v,
    b1s, b1r, bzs, bzr, b2s, b2r,
    pall, pr, qs, rla, rlb, fl, fr,
    lsem, agx_s, agx_r, agd_s, agd_r,
    y1_ss, y1_rs, m1_ss, m1_rs, z_ss, z_rs, mz_ss, mz_rs, y2_ss, y2_rs,
    b1_ss, b1_rs, bz_ss, bz_rs, b2_ss, b2_rs,
    d_ss, d_rs, rx_ss, rx_rs,
):
    seq = lax.axis_index("seq")
    head = lax.axis_index("head")
    z, y = seq // NY, seq % NY
    xx, core = head // 2, head % 2
    x_at = lambda k: (xx + k) % NX

    def dev(seq_id, head_id):
        return {"seq": seq_id, "head": head_id}

    right = dev(seq, x_at(1) * 2 + core)
    left = dev(seq, x_at(3) * 2 + core)
    partner = dev(seq, xx * 2 + 1 - core)
    y_peer = lambda r: dev(z * NY + (y + r) % NY, head)
    z_peer = lambda r: dev(((z + r) % NZ) * NY + y, head)

    def remote(src, dst, ss, rs, to):
        return pltpu.make_async_remote_copy(
            src_ref=src, dst_ref=dst, send_sem=ss, recv_sem=rs, device_id=to, device_id_type=MESH
        )

    started = []

    def send(*args):
        copy = remote(*args)
        copy.start()
        started.append(copy)

    sent_where = []

    def send_where(condition, *args):
        copy = remote(*args)
        pl.when(condition)(copy.start)
        sent_where.append((condition, copy))

    own_rows = pl.ds(pl.multiple_of(head * Q, Q), Q)
    loads = [
        pltpu.make_async_copy(x_hbm, x_v, lsem.at[0]),
        pltpu.make_async_copy(wk_hbm, wk, lsem.at[1]),
        pltpu.make_async_copy(rk_hbm, rk, lsem.at[2]),
        pltpu.make_async_copy(g_hbm, g_v, lsem.at[3]),
        pltpu.make_async_copy(go_hbm, go_v.at[own_rows, :], lsem.at[4]),
        pltpu.make_async_copy(wo_hbm, wo_v, lsem.at[5]),
    ]

    zr[...] = jnp.zeros_like(zr)
    bzr[...] = jnp.zeros_like(bzr)
    barrier = pltpu.get_barrier_semaphore()
    peers = [right, left, partner]
    peers += [y_peer(r) for r in Y_STEPS] + [z_peer(r) for r in Z_STEPS]
    for peer in peers:
        pl.semaphore_signal(barrier, inc=1, device_id=peer, device_id_type=MESH)
    for copy in loads:
        copy.start()
    pl.semaphore_wait(barrier, len(peers))

    def go_rows(place, of_core, half):
        start = pl.multiple_of((place * 2 + of_core) * Q + half * HALF, HALF)
        return go_v.at[pl.ds(start, HALF), :]

    for half in (0, 1):
        part = go_hbm.at[pl.ds(half * HALF, HALF), :]
        send(part, go_rows(xx, core, half), agx_s.at[half], agx_r.at[half], right)
        part = go_hbm.at[pl.ds((1 - half) * HALF, HALF), :]
        send(part, go_rows(xx, core, 1 - half), agx_s.at[3 - half], agx_r.at[3 - half], left)
    send(go_hbm, go_v.at[own_rows, :], agd_s.at[8], agd_r.at[8], partner)

    sub = lax.broadcasted_iota(jnp.int32, (Q, Q), 0)
    lane = lax.broadcasted_iota(jnp.int32, (Q, Q), 1)
    ones = lambda condition: condition.astype(F32).astype(BF)
    tri = ones(lane <= sub)
    eye = ones(lane == sub)
    head_lane = lax.broadcasted_iota(jnp.int32, (1, 128), 1)
    same_head = (sub % 16) == (lane % 16)
    head_of = lax.broadcasted_iota(jnp.int32, (128, WIDTH), 1) // HP
    spread_v[...] = ones(head_of == lax.broadcasted_iota(jnp.int32, (128, WIDTH), 0) % 16)
    m_lo = ones(head_lane < HP)
    m_hi = ones(head_lane >= HP)

    def in_block(c):
        return ones(head_lane // 16 == c)

    def expand_row(w):
        w = jnp.where(head_lane < 16, w, 0.0)
        a = w.astype(BF)
        return dot(a, spread_v[...]) + dot((w - a.astype(F32)).astype(BF), spread_v[...])

    def rows_of(c):
        return pl.ds(pl.multiple_of(c * Q, Q), Q)

    ldp_v[...] = jnp.zeros_like(ldp_v)
    for c in range(CHUNKS):
        ldp_v[16 * c : 16 * c + HEADS, :] = ld[:, c * Q : (c + 1) * Q] * LOG2E
        docm_v[16 * c : 16 * c + 16, :] = jnp.broadcast_to(docs[c : c + 1, :].astype(F32), (16, Q))
    parts = split3(ldp_v[...])
    ccol_all = sum(dot_nt(tri, part) for part in parts)
    ccol_v[...] = ccol_all
    dt_all = dot_nt(eye, docm_v[...].astype(BF))
    c_end, d_end = ccol_all[Q - 1 : Q, :], dt_all[Q - 1 : Q, :]
    df = jnp.broadcast_to(docm_v[0:1, 0:1], (1, 128))
    dl = jnp.broadcast_to(docm_v[127:128, 127:128], (1, 128))
    end_parts = split3(jnp.broadcast_to(c_end, (8, 128)))
    before = ones(same_head & (sub // 16 < lane // 16))
    off = sum(dot(part, before) for part in end_parts)[0:1, :]
    total = sum(dot(part, ones(same_head)) for part in end_parts)[0:1, :]
    prev = jnp.where(head_lane < 16, df, pltpu.roll(d_end, 16, 1))
    w_exs = jnp.where(dt_all == dl, jnp.exp2(total - off - ccol_all), 0.0).astype(BF)

    def ag_rows(unit, of_core):
        if unit < 4:
            return go_rows(x_at((3, 3, 1, 1)[unit]), of_core, unit % 2)
        start = (x_at(2) * 2 + of_core) * Q + (unit - 4) * (HALF // 2)
        return go_v.at[pl.ds(pl.multiple_of(start, HALF // 2), HALF // 2), :]

    def ag_got(unit):
        ref = ag_rows(unit, core)
        remote(ref, ref, agx_s.at[unit], agx_r.at[unit], left).wait_recv()
        if unit in (0, 3):
            place, to = (x_at(3), right) if unit == 0 else (x_at(1), left)
            for piece in (0, 1):
                start = (place * 2 + core) * Q + (unit % 2) * HALF + piece * (HALF // 2)
                rows = pl.ds(pl.multiple_of(start, HALF // 2), HALF // 2)
                far = 4 + (unit % 2) * 2 + piece
                send(go_v.at[rows, :], go_v.at[rows, :], agx_s.at[far], agx_r.at[far], to)
        send(ref, ref, agd_s.at[unit], agd_r.at[unit], partner)

    def ag_pair_got(unit):
        ref = ag_rows(unit, 1 - core)
        remote(ref, ref, agd_s.at[unit], agd_r.at[unit], partner).wait_recv()

    m1s[...] = stacked([total, df, dl], 8)
    m1r[y] = m1s[...]
    for r in Y_STEPS:
        send(m1s, m1r.at[y], m1_ss.at[r], m1_rs.at[r], y_peer(r))

    loads[0].wait()
    for c in range(CHUNKS):
        rows = slice(c * Q, (c + 1) * Q)
        exs = dot(w_exs * in_block(c), spread_v[...]).astype(BF)
        exs_v[rows, :] = exs
        dy_v[rows, :] = x_v[rows, :] * exs
    loads[1].wait()
    y1s[...] = dot_tn(wk[...], dy_v[...]).astype(BF)
    own_q = pl.ds(pl.multiple_of(y * QR, QR), QR)
    y1r[y] = y1s[own_q, :]
    for r in Y_STEPS:
        q_rows = pl.ds(pl.multiple_of(((y + r) % NY) * QR, QR), QR)
        send(y1s.at[q_rows, :], y1r.at[y], y1_ss.at[r], y1_rs.at[r], y_peer(r))

    skip_rows = [
        jnp.where(head_lane < HP, skip[2 * p], skip[2 * p + 1]) for p in range(PAIRS)
    ]

    def pair(p):
        return slice(p * 128, (p + 1) * 128)

    def doubled(v):
        return jnp.concatenate([v * m_lo, v * m_hi], axis=0)

    crow_v[...] = sum(dot_nt(part, tri) for part in parts)
    wexc_v[...] = jnp.where(dt_all == d_end, jnp.exp2(c_end - ccol_all), 0.0).astype(BF)
    wenc_v[...] = jnp.where(dt_all == prev, jnp.exp2(ccol_all), 0.0).astype(BF)
    wens_v[...] = jnp.where(dt_all == df, jnp.exp2(ccol_all + off), 0.0).astype(BF)
    block_decay = jnp.where(d_end == prev, jnp.exp2(c_end), 0.0)
    of_block = lax.broadcasted_iota(jnp.int32, (CHUNKS, 128), 0) == (
        lax.broadcasted_iota(jnp.int32, (CHUNKS, 128), 1) // 16
    )
    block_decay = jnp.where(of_block, block_decay, 0.0)
    coarse = block_decay.astype(BF)
    fine = (block_decay - coarse.astype(F32)).astype(BF)
    bd_v[...] = dot(coarse, spread_v[...]) + dot(fine, spread_v[...])
    run_v[...] = jnp.zeros_like(run_v)

    def inner_chunk(c):
        rows = rows_of(c)
        mine_only = in_block(c)
        exc = dot(wexc_v[...] * mine_only, spread_v[...]).astype(BF)
        exc_v[rows, :] = exc
        enc = dot(wenc_v[...] * mine_only, spread_v[...])
        enc_v[rows, :] = enc.astype(BF)
        ens_v[rows, :] = dot(wens_v[...] * mine_only, spread_v[...]).astype(BF)
        run = run_v[...]
        enter_v[c] = run.astype(BF)
        b, k = wk[rows, :], rk[rows, :]
        run_v[...] = run * bd_v[pl.ds(c, 1), :] + dot_tn(b, x_v[rows, :] * exc)
        ccol = pltpu.roll(ccol_v[...], (128 - 16 * c) % 128, 1)
        crow = crow_v[pl.ds(pl.multiple_of(c * 16, 16), 16), :]
        doc_row = docs[pl.ds(c, 1), :].astype(F32)
        dt = dot_nt(eye, jnp.broadcast_to(doc_row, (Q, Q)).astype(BF))
        same = dt == doc_row
        sm = jnp.where(same & (sub >= lane), dot_nt(k, b), 0.0)
        stm = jnp.where(same & (lane >= sub), dot_nt(b, k), 0.0)
        for p in range(PAIRS):
            ws, wts = [], []
            for h in (2 * p, 2 * p + 1):
                gap = ccol[:, h : h + 1] - crow[h : h + 1, :]
                ws.append((jnp.exp2(jnp.minimum(gap, 0.0)) * sm).astype(BF))
                wts.append((jnp.exp2(jnp.minimum(-gap, 0.0)) * stm).astype(BF))
            wt_v[c, p] = jnp.concatenate(wts, axis=1)
            xp = x_v[rows, pair(p)]
            mixed = dot(jnp.concatenate(ws, axis=1), doubled(xp))
            mixed += enc_v[rows, pair(p)].astype(F32) * dot(k, enter_v[c, :, pair(p)])
            mix_v[rows, pair(p)] = mixed + skip_rows[p] * xp.astype(F32)
            gate = g_v[rows, pair(p)].astype(F32)
            silu_v[rows, pair(p)] = gate / (1.0 + jnp.exp(-gate))

    loads[2].wait()
    loads[3].wait()
    pl.loop(0, 2)(inner_chunk)

    for r in Y_STEPS:
        source = (y + NY - r) % NY
        remote(m1s, m1r.at[source], m1_ss.at[r], m1_rs.at[r], y_peer(r)).wait_recv()
    meta = [m1r[j] for j in range(NY)]
    ls = [m[0:1, :] for m in meta]
    dfs = [m[1:2, :] for m in meta]
    dls = [m[2:3, :] for m in meta]

    def span(values):
        out = jnp.zeros((1, 128), F32)
        for v in values:
            out = out + v
        return out

    def gated_decay(a, b, values):
        return jnp.where(a == b, jnp.exp2(span(values)), 0.0)

    mzs[...] = stacked([span(ls), dfs[0], dls[NY - 1]], 8)
    mzr[z] = mzs[...]
    for r in Z_STEPS:
        send(mzs, mzr.at[z], mz_ss.at[r], mz_rs.at[r], z_peer(r))
    t_rows = [gated_decay(dls[j], dls[NY - 1], ls[j + 1 :]) for j in range(NY)]
    t_rows += [gated_decay(dfs[j], dfs[0], ls[:j]) for j in range(NY)]
    zrow_v[...] = expand_row(stacked(t_rows, 8))
    in_row = [(j, k) for k in range(NY) for j in range(k)]
    f_rows = [gated_decay(dls[j], dfs[k], ls[j + 1 : k]) for j, k in in_row]
    f_rows += [gated_decay(dfs[0], dfs[k], ls[:k]) for k in range(NY)]
    wrow_v[...] = expand_row(stacked(f_rows, 16))
    b_rows = [gated_decay(dfs[k], dls[j], ls[j + 1 : k]) for j, k in in_row]
    b_rows += [gated_decay(dls[NY - 1], dls[k], ls[k + 1 :]) for k in range(NY)]
    brow_v[...] = expand_row(stacked(b_rows, 16))

    pl.loop(2, 4)(inner_chunk)

    for r in Y_STEPS:
        source = (y + NY - r) % NY
        remote(y1s.at[own_q, :], y1r.at[source], y1_ss.at[r], y1_rs.at[r], y_peer(r)).wait_recv()
    zs[...] = sum(zrow_v[j : j + 1, :] * y1r[j].astype(F32) for j in range(NY)).astype(BF)
    zr[z] = zs[...]
    for r in Z_STEPS:
        send_where(z + r < NZ, zs, zr.at[z], z_ss.at[r], z_rs.at[r], z_peer(r))

    ag_got(0)
    ag_got(3)

    pl.loop(4, CHUNKS)(inner_chunk)

    loads[4].wait()
    loads[5].wait()

    def grad_mix_rows(start, count, first=False):
        rows = pl.ds(pl.multiple_of(start, Q), count)
        grad = dot_nt(go_v[rows, :], wo_v[...])
        dy = (grad * silu_v[rows, :]).astype(BF)
        dy_v[rows, :] = dy
        state = dot_tn(rk[rows, :], dy * ens_v[rows, :])
        gsum_v[...] = state if first else gsum_v[...] + state

    def grad_mix_of(place, first=False):
        grad_mix_rows(place * 2 * Q, 2 * Q, first)

    pair_own = go_v.at[pl.ds(pl.multiple_of((xx * 2 + 1 - core) * Q, Q), Q), :]
    remote(pair_own, pair_own, agd_s.at[8], agd_r.at[8], partner).wait_recv()
    grad_mix_of(xx, first=True)

    for r in Z_STEPS:
        source = (z + NZ - r) % NZ
        remote(mzs, mzr.at[source], mz_ss.at[r], mz_rs.at[r], z_peer(r)).wait_recv()
    zmeta = [mzr[i] for i in range(NZ)]
    rls = [m[0:1, :] for m in zmeta]
    rdfs = [m[1:2, :] for m in zmeta]
    rdls = [m[2:3, :] for m in zmeta]

    def flag(condition):
        return jnp.where(condition, 1.0, 0.0).astype(F32)

    zf_rows, zb_rows = [], []
    for i in range(NZ):
        gap = span([rls[m] * flag(m < z) for m in range(i + 1, NZ)])
        zf_rows.append(flag(i < z) * jnp.where(rdls[i] == dfs[0], jnp.exp2(gap), 0.0))
        gap = span([rls[m] * flag(m > z) for m in range(i)])
        zb_rows.append(flag(i > z) * jnp.where(rdfs[i] == dls[NY - 1], jnp.exp2(gap), 0.0))
    zf_v[...] = expand_row(stacked(zf_rows, 8))
    zb_v[...] = expand_row(stacked(zb_rows, 8))

    ag_got(1)
    ag_got(2)

    for r in Z_STEPS:
        source = (z + NZ - r) % NZ
        total_of = remote(zs, zr.at[source], z_ss.at[r], z_rs.at[r], z_peer(r))
        pl.when(z >= r)(total_of.wait_recv)
    row_state = sum(zf_v[i : i + 1, :] * zr[i].astype(F32) for i in range(NZ))
    for k in range(NY):
        out = wrow_v[6 + k : 7 + k, :] * row_state
        for place, (j, kk) in enumerate(in_row):
            if kk == k:
                out += wrow_v[place : place + 1, :] * y1r[j].astype(F32)
        y2s[k * QR : (k + 1) * QR, :] = out.astype(BF)
    y2r[own_q, :] = y2s[own_q, :]
    for r in Y_STEPS:
        q_rows = pl.ds(pl.multiple_of(((y + r) % NY) * QR, QR), QR)
        send(y2s.at[q_rows, :], y2r.at[own_q, :], y2_ss.at[r], y2_rs.at[r], y_peer(r))

    ag_pair_got(0)
    ag_pair_got(1)
    grad_mix_of(x_at(3))
    ag_pair_got(2)
    ag_pair_got(3)
    grad_mix_of(x_at(1))

    for r in Y_STEPS:
        source = pl.ds(pl.multiple_of(((y + NY - r) % NY) * QR, QR), QR)
        remote(y2s.at[own_q, :], y2r.at[source, :], y2_ss.at[r], y2_rs.at[r], y_peer(r)).wait_recv()

    order = [x_at(2), x_at(1), x_at(3), xx]

    def project_rows(k, start, count):
        rows = pl.ds(pl.multiple_of(order[k] * 2 * Q + start, Q), count)
        to_rows = pl.ds(pl.multiple_of(start, Q), count)
        carried = ens_v[rows, :].astype(F32) * dot(rk[rows, :], y2r[...])
        gated = ((mix_v[rows, :] + carried) * silu_v[rows, :]).astype(BF)
        for n in range(5):
            cols = slice(n * 512, (n + 1) * 512)
            pall[k, to_rows, cols] = dot(gated, wo_v[:, cols]).astype(BF)

    def pair_copy(k, half, of_core):
        rows = pl.ds(pl.multiple_of(of_core * Q + half * HALF, HALF), HALF)
        to_rows = pl.ds(half * HALF, HALF)
        place = 2 * k + half
        return pall.at[k, rows, :], pr.at[k, to_rows, :], d_ss.at[place], d_rs.at[place], partner

    def to_partner(k, halves):
        for half in halves:
            send(*pair_copy(k, half, 1 - core))

    def project(k, halves):
        project_rows(k, 0, 2 * Q)
        to_partner(k, halves)

    def pair_sum(k, start, count):
        rows = pl.ds(pl.multiple_of(core * Q + start, HALF), count)
        return pall[k, rows, :].astype(F32) + pr[k, start : start + count, :].astype(F32)

    def pair_got(k, half):
        remote(*pair_copy(k, half, core)).wait_recv()

    def half(ref, which):
        return ref.at[pl.ds(which * HALF, HALF), :]

    project_rows(0, (1 - core) * Q, Q)
    to_partner(0, (0, 1))
    project_rows(0, core * Q, Q)
    for unit in (4, 6, 5, 7):
        ag_got(unit)
    project(1, (1, 0))
    for which, to, landing in ((0, right, rla), (1, left, rlb)):
        pair_got(0, which)
        rows = slice(which * HALF, (which + 1) * HALF)
        qs[0, rows, :] = pair_sum(0, which * HALF, HALF).astype(BF)
        send(half(qs.at[0], which), landing, rx_ss.at[which], rx_rs.at[which], to)

    for unit in (4, 6, 5, 7):
        ag_pair_got(unit)
    grad_mix_of(x_at(2))
    b1s[...] = gsum_v[...].astype(BF)
    b1r[y] = b1s[own_q, :]
    for r in Y_STEPS:
        q_rows = pl.ds(pl.multiple_of(((y + r) % NY) * QR, QR), QR)
        send(b1s.at[q_rows, :], b1r.at[y], b1_ss.at[r], b1_rs.at[r], y_peer(r))

    pair_got(1, 1)
    qs[1, HALF:Q, :] = pair_sum(1, HALF, HALF).astype(BF)
    send(half(qs.at[1], 1), half(fl, 1), rx_ss.at[2], rx_rs.at[2], right)
    project(2, (0, 1))
    project(3, (0, 1))
    pair_got(2, 0)
    qs[2, 0:HALF, :] = pair_sum(2, 0, HALF).astype(BF)
    send(half(qs.at[2], 0), half(fr, 0), rx_ss.at[3], rx_rs.at[3], left)

    def relay():
        remote(half(qs.at[0], 0), rla, rx_ss.at[0], rx_rs.at[0], right).wait_recv()
        pair_got(1, 0)
        qs[1, 0:HALF, :] = (pair_sum(1, 0, HALF) + rla[...].astype(F32)).astype(BF)
        send(half(qs.at[1], 0), half(fl, 0), rx_ss.at[4], rx_rs.at[4], right)
        remote(half(qs.at[0], 1), rlb, rx_ss.at[1], rx_rs.at[1], left).wait_recv()
        pair_got(2, 1)
        qs[2, HALF:Q, :] = (pair_sum(2, HALF, HALF) + rlb[...].astype(F32)).astype(BF)
        send(half(qs.at[2], 1), half(fr, 1), rx_ss.at[5], rx_rs.at[5], left)

    run_v[...] = jnp.zeros_like(run_v)

    def grad_chunk(back):
        c = CHUNKS - 1 - back
        rows = rows_of(c)
        b = wk[rows, :]
        run = run_v[...]
        run_v[...] = bd_v[pl.ds(c, 1), :] * run + dot_tn(rk[rows, :], dy_v[rows, :] * enc_v[rows, :])
        arr = run.astype(BF)
        arr_v[...] = arr
        for p in range(PAIRS):
            dyp = dy_v[rows, pair(p)]
            grad = dot(wt_v[c, p], doubled(dyp))
            grad += exc_v[rows, pair(p)].astype(F32) * dot(b, arr_v[:, pair(p)])
            gl_v[rows, pair(p)] = grad + skip_rows[p] * dyp.astype(F32)

    pl.loop(0, 4)(grad_chunk)

    for r in Y_STEPS:
        source = (y + NY - r) % NY
        remote(b1s.at[own_q, :], b1r.at[source], b1_ss.at[r], b1_rs.at[r], y_peer(r)).wait_recv()
    bzs[...] = sum(
        zrow_v[NY + j : NY + j + 1, :] * b1r[j].astype(F32) for j in range(NY)
    ).astype(BF)
    bzr[z] = bzs[...]
    for r in Z_STEPS:
        send_where(z + r >= NZ, bzs, bzr.at[z], bz_ss.at[r], bz_rs.at[r], z_peer(r))

    relay()
    pl.loop(4, CHUNKS)(grad_chunk)

    for r in Z_STEPS:
        source = (z + NZ - r) % NZ
        total_of = remote(bzs, bzr.at[source], bz_ss.at[r], bz_rs.at[r], z_peer(r))
        pl.when(z < r)(total_of.wait_recv)
    row_state = sum(zb_v[i : i + 1, :] * bzr[i].astype(F32) for i in range(NZ))
    for k in range(NY):
        out = brow_v[6 + k : 7 + k, :] * row_state
        for place, (kk, j) in enumerate(in_row):
            if kk == k:
                out += brow_v[place : place + 1, :] * b1r[j].astype(F32)
        b2s[k * QR : (k + 1) * QR, :] = out.astype(BF)
    b2r[own_q, :] = b2s[own_q, :]
    for r in Y_STEPS:
        q_rows = pl.ds(pl.multiple_of(((y + r) % NY) * QR, QR), QR)
        send(b2s.at[q_rows, :], b2r.at[own_q, :], b2_ss.at[r], b2_rs.at[r], y_peer(r))

    pair_got(3, 0)
    pair_got(3, 1)
    qs[3] = pair_sum(3, 0, Q).astype(BF)

    for r in Y_STEPS:
        source = pl.ds(pl.multiple_of(((y + NY - r) % NY) * QR, QR), QR)
        remote(b2s.at[own_q, :], b2r.at[source, :], b2_ss.at[r], b2_rs.at[r], y_peer(r)).wait_recv()

    @pl.loop(0, CHUNKS // 2)
    def _(k):
        rows = pl.ds(pl.multiple_of(k * 2 * Q, 2 * Q), 2 * Q)
        carried = exs_v[rows, :].astype(F32) * dot(wk[rows, :], b2r[...])
        gi[rows, :] = (gl_v[rows, :] + carried).astype(BF)

    remote(half(qs.at[1], 1), half(fl, 1), rx_ss.at[2], rx_rs.at[2], right).wait_recv()
    remote(half(qs.at[2], 0), half(fr, 0), rx_ss.at[3], rx_rs.at[3], left).wait_recv()
    remote(half(qs.at[1], 0), half(fl, 0), rx_ss.at[4], rx_rs.at[4], right).wait_recv()
    remote(half(qs.at[2], 1), half(fr, 1), rx_ss.at[5], rx_rs.at[5], left).wait_recv()
    mo[...] = (qs[3].astype(F32) + fl[...].astype(F32) + fr[...].astype(F32)).astype(BF)

    for copy in started:
        copy.wait_send()
    for condition, copy in sent_where:
        pl.when(condition)(copy.wait_send)


def write_out(mo, gi, mo_out, gi_out, sem):
    copies = []
    for ref, out in ((mo, mo_out), (gi, gi_out)):
        count = ref.shape[0] // 4
        for k in range(4):
            rows = pl.ds(k * count, count)
            place = sem.at[len(copies)]
            copies.append(pltpu.make_async_copy(ref.at[rows, :], out.at[rows, :], place))
    for copy in copies:
        copy.start()
    for copy in copies:
        copy.wait()


def shards(
    inputs, gates, write_keys, read_keys, log_decay, skip_gain, doc_ids, out_weight, grad_out
):
    vmem = pl.BlockSpec(memory_space=pltpu.VMEM)
    smem = pl.BlockSpec(memory_space=pltpu.SMEM)
    hbm = pl.BlockSpec(memory_space=pl.ANY)
    v = lambda shape, kind=BF: pltpu.VMEM(shape, kind)
    dma = lambda *shape: pltpu.SemaphoreType.DMA(shape)
    full, square = (TOK, WIDTH), (128, 128)
    scratch = [
        v(full), v(full), v((TOK, N)), v((TOK, N)), v((WIDTH, D)), v((TOK, D)),
        v(full, F32), v(full, F32), v(full, F32),
        v(full), v(full), v(full), v(full), v((CHUNKS, PAIRS, Q, 2 * Q)), v(full),
        v((CHUNKS, N, WIDTH)), v((N, WIDTH)), v((N, WIDTH), F32),
        v((N, WIDTH), F32), v(square, F32), v(square, F32), v(square, F32), v(square, F32),
        v(square), v(square), v(square), v((CHUNKS, WIDTH), F32),
        v((128, WIDTH)),
        v((N, WIDTH)), v((NY, QR, WIDTH)), v((8, 128), F32), v((NY, 8, 128), F32),
        v((QR, WIDTH)), v((NZ, QR, WIDTH)), v((8, 128), F32), v((NZ, 8, 128), F32),
        v((N, WIDTH)), v((N, WIDTH)), v((16, WIDTH), F32), v((16, WIDTH), F32),
        v((8, WIDTH), F32), v((8, WIDTH), F32), v((8, WIDTH), F32),
        v((N, WIDTH)), v((NY, QR, WIDTH)), v((QR, WIDTH)), v((NZ, QR, WIDTH)),
        v((N, WIDTH)), v((N, WIDTH)),
        v((NX, 2 * Q, D)), v((NX, Q, D)), v((NX, Q, D)), v((HALF, D)), v((HALF, D)),
        v((Q, D)), v((Q, D)),
        dma(6), dma(8), dma(8), dma(9), dma(9),
        dma(NY), dma(NY), dma(NY), dma(NY), dma(NZ), dma(NZ), dma(NZ), dma(NZ), dma(NY), dma(NY),
        dma(NY), dma(NY), dma(NZ), dma(NZ), dma(NY), dma(NY),
        dma(8), dma(8), dma(6), dma(6),
    ]
    results = pl.pallas_call(
        kernel,
        out_shape=(pltpu.VMEM((Q, D), BF), pltpu.VMEM((TOK, WIDTH), BF)),
        in_specs=[hbm, hbm, hbm, hbm, vmem, smem, vmem, hbm, hbm],
        out_specs=(vmem, vmem),
        scratch_shapes=scratch,
        compiler_params=pltpu.CompilerParams(
            collective_id=0, has_side_effects=True, vmem_limit_bytes=54 * 1024 * 1024
        ),
    )(
        inputs, gates, write_keys, read_keys, log_decay, skip_gain,
        doc_ids.reshape(CHUNKS, Q), out_weight, grad_out,
    )
    return pl.pallas_call(
        write_out,
        out_shape=(
            jax.ShapeDtypeStruct((Q, D), BF),
            jax.ShapeDtypeStruct((TOK, WIDTH), BF),
        ),
        in_specs=[vmem, vmem],
        out_specs=(hbm, hbm),
        scratch_shapes=[dma(8)],
        compiler_params=pltpu.CompilerParams(vmem_limit_bytes=1024 * 1024),
    )(*results)


def solution(mesh):
    return jax.shard_map(
        shards,
        mesh=mesh,
        in_specs=(
            P("seq", "head"),
            P("seq", "head"),
            P("seq", None),
            P("seq", None),
            P("head", "seq"),
            P("head"),
            P("seq"),
            P("head", None),
            P(("seq", "head"), None),
        ),
        out_specs=(P(("seq", "head"), None), P("seq", "head")),
        check_vma=False,
    )
```
